1024 devices in a mesh: dom: 128 (over x, z, core), sub: 8 (over y).
Axes of the slice: x: 4, y: 8, z: 16, core: 2. Of those that a mesh axis runs over, the one named last changes fastest.
Arguments:
- solution: float32 [56, 9, 16384], P(None, None, ('dom', 'sub')), may hold values from -1.5 to 1.5
- stiffness: float32 [3, 56, 56], replicated, may hold values from -0.75 to 0.75
- star_matrices: float32 [3, 9, 9, 16384], P(None, None, None, ('dom', 'sub')), may hold values from -4.3 to 4.3
- face_restrict: float32 [4, 21, 56], replicated, may hold values from -0.75 to 0.75
- face_lift: float32 [4, 56, 21], replicated, may hold values from -1.25 to 1.25
- orient_maps: float32 [3, 21, 21], replicated, may hold values from -1.25 to 1.25
- flux_local: float32 [4, 9, 9, 16384], P(None, None, None, ('dom', 'sub')), may hold values from -1 to 1
- flux_remote: float32 [4, 9, 9, 16384], P(None, None, None, ('dom', 'sub')), may hold values from -1 to 1
- cluster_rate: int32 [16384], P(('dom', 'sub')), may hold values from 1 to 2, as said below
- send_list: int32 [1024, 4, 4], P(('dom', 'sub')), may hold values from 0 to 15, as said below
- neighbour_slot: int32 [4, 16384], P(None, ('dom', 'sub')), may hold values from 0 to 31, as said below
- neighbour_face: int32 [4, 16384], P(None, ('dom', 'sub')), may hold values from 0 to 3
- neighbour_turn: int32 [4, 16384], P(None, ('dom', 'sub')), may hold values from 0 to 2
Outputs:
- new_solution: float32 [56, 9, 16384], P(None, None, ('dom', 'sub'))
The draws below stay inside these ranges and needn't reach their ends.
Inputs may be any that keep to these rules, and one draw needn't show every extreme that they name: `cluster_rate`: 1 is the slow cluster, 2 the fast one. Among the 16 elements of one device at most 8 are fast, and some device has exactly 8. `send_list`: row p of a device's lists names elements of that device sent toward neighbour p (0: previous along dom, 1: next along dom, 2: previous along sub, 3: next along sub, cyclically); the four rows of a device hold each of its 16 elements exactly once. In every row the fast elements stand before the slow ones, at most 2 of them, and some row has exactly 2. `neighbour_slot`: A value below 16 names an element of the same device; the value 16 + p * 4 + k names the k-th element received from neighbour p, and each of these 16 values appears exactly once among one device's faces.
All inputs are finite; a program needn't handle non-finite values.
Results may differ from the reference program's by a relative error of at most 0.0001.
Values sent between devices are 32-bit elements; how exact they have to be, the bound alone decides.
A program may use at most 64 MiB of HBM per device.

```python
import math
import jax
import jax.numpy as jnp
from jax import lax

MODES = 56
FACE_MODES = 21
FIELDS = 9
DERIVS = 6
E_DEV = 16
SEND = 4
FAST_MAX = 8
E_TOTAL = 16384
N_DOM = 128
N_SUB = 8
DEVICES = 1024


def cluster_layout(key):
    key_shift, key_pick, key_slots, key_order = jax.random.split(jax.random.fold_in(key, 11), 4)
    halvings = jax.random.randint(key_shift, (DEVICES,), 0, 4)
    busiest = jax.random.randint(key_pick, (), 0, DEVICES)
    halvings = jnp.where(jnp.arange(DEVICES) == busiest, 0, halvings)
    fast_count = jnp.right_shift(jnp.full((DEVICES,), FAST_MAX, jnp.int32), halvings.astype(jnp.int32))
    leading = SEND // 2
    slot_keys = jax.random.split(key_slots, DEVICES)
    capable = jax.vmap(lambda one_key: jax.random.permutation(one_key, 4 * leading))(slot_keys)
    chosen = (capable < fast_count[:, None]).reshape(DEVICES, 4, leading).astype(jnp.int32)
    row_fast = jnp.sum(chosen, axis=2).astype(jnp.int32)
    row_slow = (SEND - row_fast).astype(jnp.int32)
    fast_start = jnp.cumsum(row_fast, axis=1) - row_fast
    slow_start = jnp.cumsum(row_slow, axis=1) - row_slow
    position = jnp.arange(SEND, dtype=jnp.int32)[None, None, :]
    is_fast = position < row_fast[:, :, None]
    pick = jnp.where(is_fast, fast_start[:, :, None] + position, fast_count[:, None, None] + slow_start[:, :, None] + position - row_fast[:, :, None])
    order_keys = jax.random.split(key_order, DEVICES)
    elements = jax.vmap(lambda one_key: jax.random.permutation(one_key, E_DEV))(order_keys).astype(jnp.int32)
    send = jnp.take_along_axis(elements, pick.reshape(DEVICES, -1).astype(jnp.int32), axis=1)
    send = send.reshape(DEVICES, 4, SEND).astype(jnp.int32)
    inverse = jnp.argsort(elements, axis=1)
    cluster = jnp.where(inverse < fast_count[:, None], 2, 1)
    return (cluster.reshape(-1).astype(jnp.int32), send)


def draw_cluster_rate(key, part):
    cluster, send = cluster_layout(key)
    return cluster


def draw_send_list(key, part):
    cluster, send = cluster_layout(key)
    return send


def draw_neighbour_slot(key, part):
    key_place, key_local = jax.random.split(jax.random.fold_in(key, 37))
    place_keys = jax.random.split(key_place, DEVICES)
    placement = jax.vmap(lambda one_key: jax.random.permutation(one_key, 4 * E_DEV))(place_keys)
    local_pick = jax.random.randint(key_local, (DEVICES, 4 * E_DEV), 0, E_DEV)
    slots = jnp.where(placement < 4 * SEND, E_DEV + placement, local_pick)
    slots = slots.reshape(DEVICES, 4, E_DEV).transpose(1, 0, 2).reshape(4, DEVICES * E_DEV)
    return slots.astype(jnp.int32)


def plant(values, own_key, smallest, top_value):
    dims = values.shape
    spot = [jax.random.randint(jax.random.fold_in(own_key, axis), (), 0, dims[axis]) for axis in range(len(dims))]
    values = values.at[tuple(spot)].set(smallest)
    longest = dims.index(max(dims))
    spot[longest] = (spot[longest] + 1) % dims[longest]
    return values.at[tuple(spot)].set(top_value)


def steps_of(stream_key, shape, shards, low, top_value):
    def one(dim, blocks):
        draws = jax.random.uniform(jax.random.fold_in(jax.random.fold_in(stream_key, 6), dim), (blocks,), jnp.float32, low / len(shards), top_value / len(shards))
        return jnp.repeat(jnp.exp(draws), shape[dim] // blocks).reshape((-1,) + (1,) * (len(shape) - dim - 1))

    factor_of = one(*shards[0])
    for cut in shards[1:]:
        factor_of = factor_of * one(*cut)
    return factor_of


def centred(rng, extent, width, reach, cuts=(), kind=jnp.bfloat16):
    entries = jax.random.normal(rng, extent, jnp.float32) * width
    if len(cuts) > 0:
        entries = steps_of(rng, extent, cuts, -0.22, 0.18) * entries
    return jnp.clip(entries, min=-reach, max=reach).astype(kind)


def setup_inputs(seed: int = 0) -> dict:
    key_list = jax.random.split(jax.random.key(seed), 14)
    return {
        "solution": centred(key_list[0], (MODES, FIELDS, E_TOTAL), 0.25, 1.5, ((2, 1024),), jnp.float32),
        "stiffness": centred(key_list[1], (3, MODES, MODES), MODES ** -0.5, 0.75, (), jnp.float32),
        "star_matrices": centred(key_list[2], (3, FIELDS, FIELDS, E_TOTAL), 0.72, 4.3, ((3, 1024),), jnp.float32),
        "face_restrict": centred(key_list[3], (4, FACE_MODES, MODES), MODES ** -0.5, 0.75, (), jnp.float32),
        "face_lift": centred(key_list[4], (4, MODES, FACE_MODES), FACE_MODES ** -0.5, 1.25, (), jnp.float32),
        "orient_maps": centred(key_list[5], (3, FACE_MODES, FACE_MODES), FACE_MODES ** -0.5, 1.25, (), jnp.float32),
        "flux_local": centred(key_list[6], (4, FIELDS, FIELDS, E_TOTAL), (4 * FIELDS) ** -0.5, 1.0, ((3, 1024),), jnp.float32),
        "flux_remote": centred(key_list[7], (4, FIELDS, FIELDS, E_TOTAL), (4 * FIELDS) ** -0.5, 1.0, ((3, 1024),), jnp.float32),
        "cluster_rate": draw_cluster_rate(jax.random.fold_in(key_list[13], 71), 0),
        "send_list": draw_send_list(jax.random.fold_in(key_list[13], 71), 0),
        "neighbour_slot": draw_neighbour_slot(jax.random.fold_in(key_list[13], 71), 0),
        "neighbour_face": plant(jax.random.randint(key_list[11], (4, E_TOTAL), 0, 4), jax.random.fold_in(key_list[11], 1), 0, 3).astype(jnp.int32),
        "neighbour_turn": plant(jax.random.randint(key_list[12], (4, E_TOTAL), 0, 3), jax.random.fold_in(key_list[12], 1), 0, 2).astype(jnp.int32),
    }


highest = lax.Precision.HIGHEST


def matrix_apply(matrix, values):
    flattened = values.reshape(values.shape[0], -1)
    product = jnp.dot(matrix, flattened, precision=highest, preferred_element_type=jnp.float32)
    return product.reshape((matrix.shape[0],) + values.shape[1:])


def star_apply(values, coupling):
    result = values[:, 0:1, :] * coupling[0][None]
    for column in range(1, coupling.shape[0]):
        result = result + values[:, column:column + 1, :] * coupling[column][None]
    return result


def derive(values, stiffness, star_matrices):
    result = star_apply(matrix_apply(stiffness[0], values), star_matrices[0])
    for axis_dir in range(1, 3):
        result = result + star_apply(matrix_apply(stiffness[axis_dir], values), star_matrices[axis_dir])
    return -result


def taylor_weight(lower, upper, degree):
    return (upper ** (degree + 1) - lower ** (degree + 1)) / math.factorial(degree + 1)


def predict(values, stiffness, star_matrices):
    current = values
    early_part = taylor_weight(0.0, 0.5, 0) * current
    late_part = taylor_weight(0.5, 1.0, 0) * current
    for degree in range(1, DERIVS):
        current = derive(current, stiffness, star_matrices)
        early_part = early_part + taylor_weight(0.0, 0.5, degree) * current
        late_part = late_part + taylor_weight(0.5, 1.0, degree) * current
    return early_part, late_part


def trace_all(operators, values):
    stacked = operators.reshape(-1, operators.shape[2])
    product = matrix_apply(stacked, values)
    return product.reshape((operators.shape[0], operators.shape[1]) + values.shape[1:])


def pick_code(stacked, code, count):
    result = jnp.where((code == 0)[None, None, :], stacked[0], 0.0)
    for option_index in range(1, count):
        result = result + jnp.where((code == option_index)[None, None, :], stacked[option_index], 0.0)
    return result


def volume_term(values, stiffness, star_part):
    result = star_apply(matrix_apply(stiffness[0].T, values), star_part[0])
    for axis_dir in range(1, 3):
        result = result + star_apply(matrix_apply(stiffness[axis_dir].T, values), star_part[axis_dir])
    return result


def local_flux(own_traces, face_lift, local_part):
    result = matrix_apply(face_lift[0], star_apply(own_traces[0], local_part[0]))
    for face_index in range(1, 4):
        result = result + matrix_apply(face_lift[face_index], star_apply(own_traces[face_index], local_part[face_index]))
    return result


def oriented_flux(gathered, face_code, turn_code, face_index, face_lift, orient_maps, remote_part):
    chosen = pick_code(gathered, face_code, 4)
    turned = pick_code(trace_all(orient_maps, chosen), turn_code, 3)
    return matrix_apply(face_lift[face_index], star_apply(turned, remote_part[face_index]))


def remote_flux(integral, global_rows, neighbour_face, neighbour_turn, face_restrict, face_lift, orient_maps, flux_remote):
    result = None
    for face_index in range(4):
        gathered = trace_all(face_restrict, jnp.take(integral, global_rows[face_index], axis=2))
        contribution = oriented_flux(gathered, neighbour_face[face_index], neighbour_turn[face_index], face_index, face_lift, orient_maps, flux_remote)
        result = contribution if result is None else result + contribution
    return result


def advance(base, own, remote, stiffness, star_matrices, face_restrict, face_lift, flux_local):
    own_traces = trace_all(face_restrict, own)
    return base + volume_term(own, stiffness, star_matrices) - local_flux(own_traces, face_lift, flux_local) - remote


def global_neighbours(neighbour_slot, send_list, owner_device):
    ghost_index = neighbour_slot - E_DEV
    remote_flag = ghost_index >= 0
    ghost_index = jnp.maximum(ghost_index, 0)
    peer_side = ghost_index // SEND
    slot_index = ghost_index % SEND
    owners = jnp.broadcast_to(owner_device[None, :], neighbour_slot.shape)
    dom_place = owners // N_SUB
    sub_place = owners % N_SUB
    dom_peer = (dom_place + jnp.where(peer_side == 0, -1, jnp.where(peer_side == 1, 1, 0))) % N_DOM
    sub_peer = (sub_place + jnp.where(peer_side == 2, -1, jnp.where(peer_side == 3, 1, 0))) % N_SUB
    peer_device = (dom_peer * N_SUB + sub_peer).astype(jnp.int32)
    sent_element = send_list[peer_device, jnp.bitwise_xor(peer_side, 1), slot_index]
    local_rows = owners * E_DEV + neighbour_slot
    return jnp.where(remote_flag, peer_device * E_DEV + sent_element, local_rows).astype(jnp.int32)


def reference(solution, stiffness, star_matrices, face_restrict, face_lift, orient_maps, flux_local, flux_remote, cluster_rate, send_list, neighbour_slot, neighbour_face, neighbour_turn):
    owner_device = (jnp.arange(solution.shape[2], dtype=jnp.int32) // E_DEV).astype(jnp.int32)
    global_rows = global_neighbours(neighbour_slot, send_list, owner_device)
    fast_flag = (cluster_rate == 2)[None, None, :]
    early_part, late_part = predict(solution, stiffness, star_matrices)
    early_remote = remote_flux(early_part, global_rows, neighbour_face, neighbour_turn, face_restrict, face_lift, orient_maps, flux_remote)
    middle = advance(solution, early_part, early_remote, stiffness, star_matrices, face_restrict, face_lift, flux_local)
    restart, unused_part = predict(middle, stiffness, star_matrices)
    late_value = jnp.where(fast_flag, restart, late_part)
    late_remote = remote_flux(late_value, global_rows, neighbour_face, neighbour_turn, face_restrict, face_lift, orient_maps, flux_remote)
    fast_end = advance(middle, late_value, late_remote, stiffness, star_matrices, face_restrict, face_lift, flux_local)
    whole_part = early_part + late_value
    whole_remote = remote_flux(whole_part, global_rows, neighbour_face, neighbour_turn, face_restrict, face_lift, orient_maps, flux_remote)
    slow_end = advance(solution, whole_part, whole_remote, stiffness, star_matrices, face_restrict, face_lift, flux_local)
    return jnp.where(fast_flag, fast_end, slow_end)
```

```python
import math

import jax
import jax.numpy as jnp
from jax import lax
from jax.experimental import pallas as pl
from jax.experimental.pallas import tpu as pltpu
from jax.sharding import PartitionSpec as P

MODES = 56
FACE_MODES = 21
FIELDS = 9
DERIVS = 6
E_DEV = 16
EVERY = FIELDS * FIELDS
MESH = pl.DeviceIdType.MESH
F32 = jnp.float32
BF16 = jnp.bfloat16


def taylor_weight(lower, upper, degree):
    return (upper ** (degree + 1) - lower ** (degree + 1)) / math.factorial(degree + 1)


def iota(shape, axis):
    return lax.broadcasted_iota(jnp.int32, shape, axis)


def hi_lo(x):
    hi = x.astype(BF16).astype(F32)
    return hi, x - hi


def mdot(a, b):
    return jnp.dot(a, b, preferred_element_type=F32)


def twice(x):
    return x + pltpu.roll(x, 64, 1)


def lhs_of(values):
    hi, lo = hi_lo(values)
    low_half = iota(values.shape, 2) < 64
    one = jnp.where(low_half, hi, lo).reshape(values.shape[0] * values.shape[1], 128).astype(BF16)
    return jnp.concatenate([one, one], axis=1)


def store_rhs(target, value):
    hi, lo = hi_lo(value)
    target[0:128, :] = hi.astype(BF16)
    target[128:256, :] = lo.astype(BF16)


def couple(values, coefs):
    result = values[0][None] * coefs(0)
    for c in range(1, FIELDS):
        result = result + values[c][None] * coefs(c)
    return result


def couple_dirs(product, ca, cb, count):
    pair = couple(product[:, :, 0:128], lambda c: ca[c, :, 0:count, :])
    third = couple(product[:, :, 128:256], lambda c: cb[c, :, 0:count, :])
    swapped = pltpu.roll(third, 64, 2)
    low_half = iota(third.shape, 2) < 64
    even = jnp.where(low_half, third, swapped)
    odd = jnp.where(low_half, swapped, third)
    spread_third = jnp.stack([(even, odd)[j % 2][j // 2] for j in range(FIELDS)], axis=0)
    return pair + pltpu.roll(pair, 64, 2) + spread_third


def kernel(n_dom, n_sub, *refs):
    (
        send_hbm,
        sol_hbm,
        stiff_hbm,
        star_hbm,
        restrict_hbm,
        lift_hbm,
        orient_hbm,
        flocal_hbm,
        fremote_hbm,
        rate_hbm,
        slot_hbm,
        face_hbm,
        turn_hbm,
        out_ref,
        send_ref,
        sol_ref,
        stiff_ref,
        star_ref,
        restrict_ref,
        lift_ref,
        orient_ref,
        flocal_ref,
        fremote_ref,
        rate_ref,
        slot_ref,
        face_ref,
        turn_ref,
        in_sem,
        dk,
        vk,
        rt,
        qt,
        lf,
        ob,
        sq,
        tall,
        rows,
        lhs,
        ca,
        cb,
        cf,
        zs,
        ts,
        late_keep,
        base_keep,
        own_keep,
        vol_keep,
        send_a,
        send_l,
        send_b,
        recv_a,
        recv_l,
        recv_b,
        ssem,
        rsem,
    ) = refs
    dom = lax.axis_index("dom")
    sub = lax.axis_index("sub")
    peers = (
        (lax.rem(dom + n_dom - 1, n_dom), sub),
        (lax.rem(dom + 1, n_dom), sub),
        (dom, lax.rem(sub + n_sub - 1, n_sub)),
        (dom, lax.rem(sub + 1, n_sub)),
    )

    moves = [(send_hbm, send_ref), (sol_hbm, sol_ref), (stiff_hbm, stiff_ref)]
    moves += [(star_hbm.at[:, d, :], star_ref.at[d]) for d in range(3)]
    first_part = len(moves)
    moves += [(flocal_hbm.at[:, i, :], flocal_ref.at[i]) for i in range(4)]
    moves += [(fremote_hbm.at[:, i, :], fremote_ref.at[i]) for i in range(4)]
    moves += [(restrict_hbm.at[:, i, :], restrict_ref.at[i]) for i in range(4)]
    moves += [(lift_hbm.at[:, i, :], lift_ref.at[i]) for i in range(4)]
    moves += [(orient_hbm, orient_ref), (rate_hbm, rate_ref), (slot_hbm, slot_ref)]
    moves += [(face_hbm, face_ref), (turn_hbm, turn_ref)]
    loads = [
        pltpu.make_async_copy(source, target, in_sem.at[n])
        for n, (source, target) in enumerate(moves)
    ]
    for load in loads:
        load.start()

    barrier = pltpu.get_barrier_semaphore()
    for peer in peers:
        pl.semaphore_signal(barrier, inc=1, device_id=peer, device_id_type=MESH)

    def copies(source, target, which):
        return [
            pltpu.make_async_remote_copy(
                src_ref=source(p),
                dst_ref=target.at[p ^ 1],
                send_sem=ssem.at[which, p],
                recv_sem=rsem.at[which, p ^ 1],
                device_id=peers[p],
                device_id_type=MESH,
            )
            for p in range(4)
        ]

    lane16 = iota((E_DEV, 128), 1)
    sub16 = iota((E_DEV, 128), 0)
    elem_lane = lane16 & 15
    ind_k = (iota((128, 256), 0) >> 4) & 3
    ind_l = iota((128, 256), 1)
    star_ind = (ind_k == jnp.where(ind_l < 128, ind_l >> 6, 2)).astype(BF16)
    tall[...] = jnp.zeros_like(tall)
    sq[...] = jnp.zeros_like(sq)
    rows[...] = jnp.zeros_like(rows)

    for load in loads[0:first_part]:
        load.wait()

    column = jnp.zeros((E_DEV, 128), jnp.int32)
    row = jnp.zeros((E_DEV, 128), jnp.int32)
    for e in range(E_DEV):
        value = send_ref[0, e % 4, e // 4]
        column = jnp.where(sub16 == e, value, column)
        row = jnp.where(elem_lane == e, value, row)
    perm = (column == elem_lane).astype(F32)
    perm_back = (sub16 == row).astype(F32)

    def permute(matrix, values):
        hi, lo = hi_lo(values)
        stacked = jnp.concatenate([hi, lo], axis=0).astype(BF16)
        return mdot(matrix[:, 0:32].astype(BF16), stacked)

    def entry_rows(parts):
        empty = [jnp.zeros((EVERY, 16), F32)] * (4 - len(parts))
        hi, lo = hi_lo(jnp.concatenate(parts + empty, axis=1))
        return jnp.concatenate([hi, lo], axis=1)

    rows[0:EVERY, 0:128] = entry_rows([star_ref[d] for d in range(3)])
    for r in range(EVERY):
        one = jnp.broadcast_to(rows[r : r + 1, 0:128], (E_DEV, 128)) * perm
        lhs[r * E_DEV : (r + 1) * E_DEV, 0:128] = one.astype(BF16)
    product = mdot(lhs[:, 0:128], star_ind).reshape(FIELDS, FIELDS, E_DEV, 256)
    ca[...] = product[:, :, :, 0:128]
    low_cell = lane16 < 64
    for j in range(0, FIELDS, 2):
        one = product[:, j, :, 128:256]
        if j + 1 < FIELDS:
            one = jnp.where(low_cell[None], one, product[:, j + 1, :, 128:256])
        cb[:, j // 2] = one

    for d, at in ((0, 0), (1, 64), (2, 128), (2, 192)):
        tall[at : at + 56, 0:56] = -stiff_ref[d]
    for half in range(2):
        at = 128 * half
        block = jnp.transpose(twice(tall[at : at + 128, :]))
        hi, lo = hi_lo(block)
        dk[0:128, at : at + 128] = hi.astype(BF16)
        dk[128:256, at : at + 128] = lo.astype(BF16)

    state = []
    for c in range(FIELDS):
        one = jnp.concatenate([sol_ref[c], jnp.zeros((E_DEV, 72), F32)], axis=1)
        state.append(permute(perm, twice(one)))
    state = jnp.stack(state, axis=0)
    base_keep[...] = state

    def derive(values):
        count = values.shape[1]
        product = mdot(lhs_of(values), dk[...]).reshape(FIELDS, count, 256)
        return couple_dirs(product, ca, cb, count)

    current = state
    early = taylor_weight(0.0, 0.5, 0) * current
    late = taylor_weight(0.5, 1.0, 0) * current
    for degree in range(1, DERIVS):
        current = derive(current)
        early = early + taylor_weight(0.0, 0.5, degree) * current
        late = late + taylor_weight(0.5, 1.0, degree) * current
    late_keep[...] = late

    row8 = iota((5, 8, 128), 1)
    low8 = iota((5, 8, 128), 2) < 64

    def pack(values):
        return jnp.stack(
            [values[8] if q == 4 else jnp.where(low8[0], values[2 * q], values[2 * q + 1]) for q in range(5)],
            axis=0,
        )

    def unpack(values):
        other = pltpu.roll(values, 64, 2)
        even = jnp.where(low8, values, other)
        odd = jnp.where(low8, other, values)
        return jnp.stack([(even, odd)[c % 2][c // 2] for c in range(FIELDS)], axis=0)

    def whole_ghosts(source):
        side = row8 & 3
        one = jnp.where(side == 0, source[1], source[0])
        two = jnp.where(side == 2, source[3], source[2])
        return unpack(jnp.where(side < 2, one, two))

    first8, last8 = pack(early[:, 0:8, :]), pack(early[:, 8:16, :])
    upper = (row8 & 2) == 0
    send_a[0] = jnp.where(upper, first8, pltpu.roll(last8, 2, 1))
    send_a[1] = jnp.where(upper, pltpu.roll(first8, 6, 1), last8)
    pl.semaphore_wait(barrier, 4)
    exchange_a = copies(lambda p: send_a.at[p // 2], recv_a, 0)
    for copy in exchange_a:
        copy.start()
    send_l[...] = pack(late[:, 8:16, :])
    exchange_l = copies(lambda p: send_l, recv_l, 1)
    for copy in exchange_l:
        copy.start()

    for load in loads[first_part:]:
        load.wait()
    rows[0:EVERY, 0:128] = entry_rows([flocal_ref[i] for i in range(4)])
    rows[0:EVERY, 128:256] = entry_rows([fremote_ref[i] for i in range(4)])
    for r in range(EVERY):
        for half in range(2):
            at = 128 * half
            one = jnp.broadcast_to(rows[r : r + 1, at : at + 128], (E_DEV, 128)) * perm
            lhs[r * E_DEV : (r + 1) * E_DEV, at : at + 128] = one.astype(BF16)
    flux_one = ind_k == ((ind_l & 127) >> 5)
    flux_ind = jnp.concatenate(
        [(flux_one & (ind_l < 128)).astype(BF16), (flux_one & (ind_l >= 128)).astype(BF16)], axis=0
    )
    cf[...] = mdot(lhs[...], flux_ind).reshape(FIELDS, FIELDS, E_DEV, 256)

    low64 = iota((64, 128), 1) < 64
    blocks = []
    for d in range(3):
        padded = jnp.concatenate([stiff_ref[d], jnp.zeros((56, 72), F32)], axis=1)
        blocks.append(jnp.concatenate([twice(padded), jnp.zeros((8, 128), F32)], axis=0))
    for part, block in enumerate((jnp.where(low64, blocks[0], blocks[1]), blocks[2])):
        at = 128 * part
        hi, lo = hi_lo(block)
        vk[0:64, at : at + 128] = hi.astype(BF16)
        vk[64:128, at : at + 128] = hi.astype(BF16)
        vk[128:192, at : at + 128] = lo.astype(BF16)
        vk[192:256, at : at + 128] = lo.astype(BF16)

    for i in range(4):
        sq[32 * i : 32 * i + 21, 0:56] = restrict_ref[i]
    traced = jnp.transpose(twice(sq[...]))
    store_rhs(rt, traced)
    for i in range(4):
        sq[32 * i : 32 * i + 21, 0:56] = lift_ref[i]
    hi, lo = hi_lo(twice(sq[...]))
    lf[0:128, :] = hi.astype(BF16)
    lf[128:256, :] = hi.astype(BF16)
    lf[256:384, :] = lo.astype(BF16)

    sq[...] = jnp.zeros_like(sq)
    for t in range(3):
        sq[21 * t : 21 * t + 21, 0:21] = orient_ref[t]
    turns = jnp.transpose(sq[...])[0:32, :]
    turns = (turns, pltpu.roll(turns, 64, 1))
    none = jnp.zeros((32, 128), F32)
    for nf in range(4):
        wide = [none, none]
        wide[nf // 2] = turns[nf % 2]
        hi, lo = hi_lo(jnp.concatenate(wide, axis=1))
        ob[32 * nf : 32 * nf + 32, :] = hi.astype(BF16)
        ob[128 + 32 * nf : 160 + 32 * nf, :] = hi.astype(BF16)
        ob[256 + 32 * nf : 288 + 32 * nf, :] = lo.astype(BF16)
    hi, lo = hi_lo(traced)
    hi, lo = hi.astype(BF16), lo.astype(BF16)
    store_rhs(qt, mdot(jnp.concatenate([hi, lo, hi], axis=1), ob[...]))

    perm16 = perm[:, 0:16]
    coded = []
    for i in range(4):
        coded.append(perm16 * slot_ref[i : i + 1, :].astype(F32))
    for i in range(4):
        coded.append(perm16 * face_ref[i : i + 1, :].astype(F32))
    for i in range(4):
        coded.append(perm16 * turn_ref[i : i + 1, :].astype(F32))
    coded.append(perm16 * rate_ref[...].astype(F32))
    codes = mdot(jnp.concatenate(coded, axis=0).astype(BF16), jnp.ones((16, 128), BF16))
    codes = codes.astype(jnp.int32)
    slots, faces, turn_of = codes[0:64, 0:64], codes[64:128], codes[128:192]
    fast = codes[192:200, :] == 2
    ghost_slot = 16 + ((elem_lane & 3) ^ 1) * 4 + (elem_lane >> 2)
    target_row = jnp.where((lane16 & 16) > 0, ghost_slot, row)
    gather = (slots == jnp.broadcast_to(target_row[0:1, 0:64], (64, 64))).astype(BF16)
    lane64 = iota((64, 128), 1)
    inner = lane64 & 63
    turn_l = (inner >= 21).astype(jnp.int32) + (inner >= 42).astype(jnp.int32)
    upper_face = faces >= 2
    mask = (((faces & 1) == (lane64 >> 6)) & (turn_of == turn_l)).astype(F32)
    place_k = iota((256, 128), 0) & 63
    place_f = place_k - 21 * ((place_k >= 21).astype(jnp.int32) + (place_k >= 42).astype(jnp.int32))
    place_l = iota((256, 128), 1)
    places = [((place_l == place_f + 32 * i) & (place_k < 63)).astype(BF16) for i in range(4)]

    def own_terms(values):
        left = lhs_of(values)
        vol_keep[...] = couple_dirs(mdot(left, vk[...]).reshape(FIELDS, E_DEV, 256), ca, cb, E_DEV)
        own = mdot(left, rt[...]).reshape(FIELDS, E_DEV, 128)
        own_keep[...] = couple(own, lambda c: cf[c, :, :, 0:128])
        hi, lo = hi_lo(mdot(left, qt[...]).reshape(FIELDS, E_DEV, 256))
        zs[:, 0:16, :] = hi.astype(BF16)
        zs[:, 32:48, :] = lo.astype(BF16)

    def ghost_terms(ghosts):
        hi, lo = hi_lo(mdot(lhs_of(ghosts), qt[...]).reshape(FIELDS, E_DEV, 256))
        zs[:, 16:32, :] = hi.astype(BF16)
        zs[:, 48:64, :] = lo.astype(BF16)
        for c in range(FIELDS):
            taken = mdot(gather, zs[c])
            taken = jnp.where(upper_face, taken[:, 128:256], taken[:, 0:128]) * mask
            hi, lo = hi_lo(taken)
            both = jnp.concatenate([hi, lo], axis=1).astype(BF16)
            for i in range(4):
                ts[i, c] = both[16 * i : 16 * i + 16, :]
        placed = mdot(ts[0].reshape(FIELDS * E_DEV, 256), places[0])
        for i in range(1, 4):
            placed = placed + mdot(ts[i].reshape(FIELDS * E_DEV, 256), places[i])
        placed = placed.reshape(FIELDS, E_DEV, 128)
        flux = own_keep[...] + couple(placed, lambda c: cf[c, :, :, 128:256])
        hi, lo = hi_lo(flux.reshape(FIELDS * E_DEV, 128))
        hi, lo = hi.astype(BF16), lo.astype(BF16)
        lifted = mdot(jnp.concatenate([hi, lo, hi], axis=1), lf[...]).reshape(FIELDS, E_DEV, 128)
        return base_keep[...] + vol_keep[...] - lifted

    own_terms(early)
    for copy in exchange_a:
        copy.wait()
    odd_row = (row8 & 1) == 1
    by_dom = jnp.where(odd_row, recv_a[0], recv_a[1])
    by_sub = jnp.where(odd_row, recv_a[2], recv_a[3])
    ghost8 = unpack(jnp.where(upper, by_dom, pltpu.roll(by_sub, 2, 1)))
    ghost16 = unpack(jnp.where(upper, pltpu.roll(by_dom, 6, 1), by_sub))
    middle = ghost_terms(jnp.concatenate([ghost8, ghost16], axis=1))
    base_keep[...] = middle

    current = middle[:, 0:8, :]
    restart = taylor_weight(0.0, 0.5, 0) * current
    for degree in range(1, DERIVS):
        current = derive(current)
        restart = restart + taylor_weight(0.0, 0.5, degree) * current
    late8 = jnp.where(fast[None], restart, late_keep[:, 0:8, :])

    send_b[...] = pack(late8)
    exchange_b = copies(lambda p: send_b, recv_b, 2)
    for copy in exchange_b:
        copy.start()
    own_terms(jnp.concatenate([late8, late_keep[:, 8:16, :]], axis=1))
    for copy in exchange_l:
        copy.wait()
    ghost16 = whole_ghosts(recv_l)
    for copy in exchange_b:
        copy.wait()
    final = ghost_terms(jnp.concatenate([whole_ghosts(recv_b), ghost16], axis=1))
    for c in range(FIELDS):
        out_ref[c] = permute(perm_back, final[c])[:, 0:56]


def solution(mesh):
    n_dom, n_sub = mesh.shape["dom"], mesh.shape["sub"]
    cells = (FIELDS, E_DEV, 128)

    def local(
        state,
        stiffness,
        star,
        face_restrict,
        face_lift,
        orient_maps,
        flux_local,
        flux_remote,
        cluster_rate,
        send_list,
        slot,
        face,
        turn,
    ):
        def entries(array):
            return jnp.transpose(array, (1, 2, 0, 3)).reshape(EVERY, array.shape[0], E_DEV)

        table = pltpu.VMEM((4, E_DEV), jnp.int32)
        out = pl.pallas_call(
            lambda *refs: kernel(n_dom, n_sub, *refs),
            out_shape=pltpu.VMEM((FIELDS, E_DEV, MODES), F32),
            in_specs=[pl.BlockSpec(memory_space=pltpu.HBM)] * 13,
            out_specs=pl.BlockSpec(memory_space=pltpu.VMEM),
            scratch_shapes=[
                pltpu.SMEM((1, 4, 4), jnp.int32),
                pltpu.VMEM((FIELDS, E_DEV, MODES), F32),
                pltpu.VMEM((3, MODES, MODES), F32),
                pltpu.VMEM((3, EVERY, E_DEV), F32),
                pltpu.VMEM((4, FACE_MODES, MODES), F32),
                pltpu.VMEM((4, FACE_MODES, MODES), F32),
                pltpu.VMEM((3, FACE_MODES, FACE_MODES), F32),
                pltpu.VMEM((4, EVERY, E_DEV), F32),
                pltpu.VMEM((4, EVERY, E_DEV), F32),
                pltpu.VMEM((1, E_DEV), jnp.int32),
                table,
                table,
                table,
                pltpu.SemaphoreType.DMA((27,)),
                pltpu.VMEM((256, 256), BF16),
                pltpu.VMEM((256, 256), BF16),
                pltpu.VMEM((256, 128), BF16),
                pltpu.VMEM((256, 256), BF16),
                pltpu.VMEM((384, 128), BF16),
                pltpu.VMEM((384, 256), BF16),
                pltpu.VMEM((128, 128), F32),
                pltpu.VMEM((256, 128), F32),
                pltpu.VMEM((88, 256), F32),
                pltpu.VMEM((EVERY * E_DEV, 256), BF16),
                pltpu.VMEM((FIELDS, FIELDS, E_DEV, 128), F32),
                pltpu.VMEM((FIELDS, 5, E_DEV, 128), F32),
                pltpu.VMEM((FIELDS, FIELDS, E_DEV, 256), F32),
                pltpu.VMEM((FIELDS, 64, 256), BF16),
                pltpu.VMEM((4, FIELDS, E_DEV, 256), BF16),
                pltpu.VMEM(cells, F32),
                pltpu.VMEM(cells, F32),
                pltpu.VMEM(cells, F32),
                pltpu.VMEM(cells, F32),
                pltpu.VMEM((2, 5, 8, 128), F32),
                pltpu.VMEM((5, 8, 128), F32),
                pltpu.VMEM((5, 8, 128), F32),
                pltpu.VMEM((4, 5, 8, 128), F32),
                pltpu.VMEM((4, 5, 8, 128), F32),
                pltpu.VMEM((4, 5, 8, 128), F32),
                pltpu.SemaphoreType.DMA((3, 4)),
                pltpu.SemaphoreType.DMA((3, 4)),
            ],
            compiler_params=pltpu.CompilerParams(
                collective_id=0, has_side_effects=True
            ),
            name="ader_step",
        )(
            send_list,
            jnp.transpose(state, (1, 2, 0)),
            stiffness,
            entries(star),
            jnp.transpose(face_restrict, (1, 0, 2)),
            jnp.transpose(face_lift, (2, 0, 1)),
            orient_maps,
            entries(flux_local),
            entries(flux_remote),
            cluster_rate.reshape(1, E_DEV),
            slot,
            face,
            turn,
        )
        return jnp.transpose(out, (2, 0, 1))

    along = ("dom", "sub")
    placed = (
        P(None, None, along),
        P(),
        P(None, None, None, along),
        P(),
        P(),
        P(),
        P(None, None, None, along),
        P(None, None, None, along),
        P(along),
        P(along, None, None),
        P(None, along),
        P(None, along),
        P(None, along),
    )
    return jax.shard_map(
        local, mesh=mesh, in_specs=placed, out_specs=P(None, None, along), check_vma=False
    )
```

```python
import math

import jax
import jax.numpy as jnp
from jax import lax
from jax.experimental import pallas as pl
from jax.experimental.pallas import tpu as pltpu
from jax.sharding import PartitionSpec as P

MODES = 56
FACE_MODES = 21
FIELDS = 9
DERIVS = 6
E_DEV = 16
EVERY = FIELDS * FIELDS
MESH = pl.DeviceIdType.MESH
F32 = jnp.float32
BF16 = jnp.bfloat16


def taylor_weight(lower, upper, degree):
    return (upper ** (degree + 1) - lower ** (degree + 1)) / math.factorial(degree + 1)


def iota(shape, axis):
    return lax.broadcasted_iota(jnp.int32, shape, axis)


def hi_lo(x):
    hi = x.astype(BF16).astype(F32)
    return hi, x - hi


def mdot(a, b):
    return jnp.dot(a, b, preferred_element_type=F32)


def twice(x):
    return x + pltpu.roll(x, 64, 1)


def lhs_of(values):
    hi, lo = hi_lo(values)
    low_half = iota(values.shape, 2) < 64
    one = jnp.where(low_half, hi, lo).reshape(values.shape[0] * values.shape[1], 128).astype(BF16)
    return jnp.concatenate([one, one[:, 0:64]], axis=1)


def store_rhs(target, value):
    hi, lo = hi_lo(value)
    target[0:128, :] = hi.astype(BF16)
    target[128:192, :] = lo[0:64].astype(BF16)


def couple(values, coefs):
    result = values[0][None] * coefs(0)
    for c in range(1, FIELDS):
        result = result + values[c][None] * coefs(c)
    return result


def couple_dirs(product, ca, cb, count):
    pair = couple(product[:, :, 0:128], lambda c: ca[c, :, 0:count, :])
    third = couple(product[:, :, 128:256], lambda c: cb[c, :, 0:count, :])
    swapped = pltpu.roll(third, 64, 2)
    low_half = iota(third.shape, 2) < 64
    even = jnp.where(low_half, third, swapped)
    odd = jnp.where(low_half, swapped, third)
    spread_third = jnp.stack([(even, odd)[j % 2][j // 2] for j in range(FIELDS)], axis=0)
    return pair + pltpu.roll(pair, 64, 2) + spread_third


def kernel(n_dom, n_sub, *refs):
    (
        send_hbm,
        sol_hbm,
        stiff_hbm,
        star_hbm,
        restrict_hbm,
        lift_hbm,
        orient_hbm,
        flocal_hbm,
        fremote_hbm,
        rate_hbm,
        slot_hbm,
        face_hbm,
        turn_hbm,
        out_ref,
        send_ref,
        sol_ref,
        stiff_ref,
        star_ref,
        restrict_ref,
        lift_ref,
        orient_ref,
        flocal_ref,
        fremote_ref,
        rate_ref,
        slot_ref,
        face_ref,
        turn_ref,
        in_sem,
        dk,
        vk,
        rt,
        qt,
        lf,
        ob,
        sq,
        tall,
        rows,
        lhs,
        ca,
        cb,
        cf,
        zs,
        deriv_keep,
        late_keep,
        base_keep,
        own_keep,
        vol_keep,
        send_a,
        send_l,
        send_b,
        recv_a,
        recv_l,
        recv_b,
        ssem,
        rsem,
    ) = refs
    dom = lax.axis_index("dom")
    sub = lax.axis_index("sub")
    peers = (
        (lax.rem(dom + n_dom - 1, n_dom), sub),
        (lax.rem(dom + 1, n_dom), sub),
        (dom, lax.rem(sub + n_sub - 1, n_sub)),
        (dom, lax.rem(sub + 1, n_sub)),
    )

    moves = [(send_hbm, send_ref), (sol_hbm, sol_ref), (stiff_hbm, stiff_ref)]
    moves += [(star_hbm.at[:, d, :], star_ref.at[d]) for d in range(3)]
    first_part = len(moves)
    moves += [(flocal_hbm.at[:, i, :], flocal_ref.at[i]) for i in range(4)]
    moves += [(fremote_hbm.at[:, i, :], fremote_ref.at[i]) for i in range(4)]
    moves += [(restrict_hbm.at[:, i, :], restrict_ref.at[i]) for i in range(4)]
    moves += [(lift_hbm.at[:, i, :], lift_ref.at[i]) for i in range(4)]
    moves += [(orient_hbm, orient_ref), (rate_hbm, rate_ref), (slot_hbm, slot_ref)]
    moves += [(face_hbm, face_ref), (turn_hbm, turn_ref)]
    loads = [
        pltpu.make_async_copy(source, target, in_sem.at[n])
        for n, (source, target) in enumerate(moves)
    ]
    for load in loads:
        load.start()

    barrier = pltpu.get_barrier_semaphore()
    for peer in peers:
        pl.semaphore_signal(barrier, inc=1, device_id=peer, device_id_type=MESH)

    def copies(source, target, which):
        return [
            pltpu.make_async_remote_copy(
                src_ref=source(p),
                dst_ref=target.at[p ^ 1],
                send_sem=ssem.at[which, p],
                recv_sem=rsem.at[which, p ^ 1],
                device_id=peers[p],
                device_id_type=MESH,
            )
            for p in range(4)
        ]

    lane16 = iota((E_DEV, 128), 1)
    sub16 = iota((E_DEV, 128), 0)
    elem_lane = lane16 & 15
    ind_k = (iota((128, 256), 0) >> 4) & 3
    ind_l = iota((128, 256), 1)
    star_ind = (ind_k == jnp.where(ind_l < 128, ind_l >> 6, 2)).astype(BF16)
    tall[...] = jnp.zeros_like(tall)
    sq[...] = jnp.zeros_like(sq)
    rows[...] = jnp.zeros_like(rows)

    for load in loads[0:first_part]:
        load.wait()

    column = jnp.zeros((E_DEV, 128), jnp.int32)
    row = jnp.zeros((E_DEV, 128), jnp.int32)
    for e in range(E_DEV):
        value = send_ref[0, e % 4, e // 4]
        column = jnp.where(sub16 == e, value, column)
        row = jnp.where(elem_lane == e, value, row)
    perm = (column == elem_lane).astype(F32)
    perm_back = (sub16 == row).astype(F32)

    def permute(matrix, values):
        hi, lo = hi_lo(values)
        stacked = jnp.concatenate([hi, lo], axis=0).astype(BF16)
        return mdot(matrix[:, 0:32].astype(BF16), stacked)

    def entry_rows(parts):
        empty = [jnp.zeros((EVERY, 16), F32)] * (4 - len(parts))
        hi, lo = hi_lo(jnp.concatenate(parts + empty, axis=1))
        return jnp.concatenate([hi, lo], axis=1)

    rows[0:EVERY, 0:128] = entry_rows([star_ref[d] for d in range(3)])
    for r in range(EVERY):
        one = jnp.broadcast_to(rows[r : r + 1, 0:128], (E_DEV, 128)) * perm
        lhs[r * E_DEV : (r + 1) * E_DEV, 0:128] = one.astype(BF16)
    product = mdot(lhs[:, 0:128], star_ind).reshape(FIELDS, FIELDS, E_DEV, 256)
    ca[...] = product[:, :, :, 0:128]
    low_cell = lane16 < 64
    for j in range(0, FIELDS, 2):
        one = product[:, j, :, 128:256]
        if j + 1 < FIELDS:
            one = jnp.where(low_cell[None], one, product[:, j + 1, :, 128:256])
        cb[:, j // 2] = one

    for d, at in ((0, 0), (1, 64), (2, 128), (2, 192)):
        tall[at : at + 56, 0:56] = -stiff_ref[d]
    for half in range(2):
        at = 128 * half
        block = jnp.transpose(twice(tall[at : at + 128, :]))
        hi, lo = hi_lo(block)
        dk[0:128, at : at + 128] = hi.astype(BF16)
        dk[128:192, at : at + 128] = lo[0:64].astype(BF16)

    state = []
    for c in range(FIELDS):
        one = jnp.concatenate([sol_ref[c], jnp.zeros((E_DEV, 72), F32)], axis=1)
        state.append(permute(perm, twice(one)))
    state = jnp.stack(state, axis=0)
    base_keep[...] = state

    def derive(values):
        count = values.shape[1]
        product = mdot(lhs_of(values), dk[...]).reshape(FIELDS, count, 256)
        return couple_dirs(product, ca, cb, count)

    current = state
    early = taylor_weight(0.0, 0.5, 0) * current
    for degree in range(1, DERIVS):
        current = derive(current)
        early = early + taylor_weight(0.0, 0.5, degree) * current
        deriv_keep[degree - 1] = current

    row8 = iota((5, 8, 128), 1)
    low8 = iota((5, 8, 128), 2) < 64

    def pack(values):
        return jnp.stack(
            [values[8] if q == 4 else jnp.where(low8[0], values[2 * q], values[2 * q + 1]) for q in range(5)],
            axis=0,
        )

    def unpack(values):
        other = pltpu.roll(values, 64, 2)
        even = jnp.where(low8, values, other)
        odd = jnp.where(low8, other, values)
        return jnp.stack([(even, odd)[c % 2][c // 2] for c in range(FIELDS)], axis=0)

    def whole_ghosts(source):
        side = row8 & 3
        one = jnp.where(side == 0, source[1], source[0])
        two = jnp.where(side == 2, source[3], source[2])
        return unpack(jnp.where(side < 2, one, two))

    upper3 = (iota((3, 8, 128), 1) & 2) == 0
    odd3 = (iota((3, 8, 128), 1) & 1) == 1

    def fast_send(values, target):
        even = jnp.stack([values[0], values[2], values[4]], axis=0)
        odd = jnp.stack([values[1], values[3], values[4]], axis=0)
        target[0] = jnp.where(upper3, even, pltpu.roll(odd, 2, 1))
        target[1] = jnp.where(upper3, pltpu.roll(even, 6, 1), odd)

    def fast_ghosts(source):
        by_dom = jnp.where(odd3, source[0], source[1])
        by_sub = jnp.where(odd3, source[2], source[3])
        even = jnp.where(upper3, by_dom, pltpu.roll(by_sub, 2, 1))
        odd = jnp.where(upper3, pltpu.roll(by_dom, 6, 1), by_sub)
        return unpack(jnp.stack([even[0], odd[0], even[1], odd[1], even[2]], axis=0))

    first8, last8 = pack(early[:, 0:8, :]), pack(early[:, 8:16, :])
    upper = (row8 & 2) == 0
    send_a[0] = jnp.where(upper, first8, pltpu.roll(last8, 2, 1))
    send_a[1] = jnp.where(upper, pltpu.roll(first8, 6, 1), last8)
    pl.semaphore_wait(barrier, 4)
    exchange_a = copies(lambda p: send_a.at[p // 2], recv_a, 0)
    for copy in exchange_a:
        copy.start()
    late = taylor_weight(0.5, 1.0, 0) * base_keep[...]
    for degree in range(1, DERIVS):
        late = late + taylor_weight(0.5, 1.0, degree) * deriv_keep[degree - 1]
    late_keep[...] = late
    send_l[...] = pack(late[:, 8:16, :])
    exchange_l = copies(lambda p: send_l, recv_l, 1)
    for copy in exchange_l:
        copy.start()

    for load in loads[first_part:]:
        load.wait()
    rows[0:EVERY, 0:128] = entry_rows([flocal_ref[i] for i in range(4)])
    rows[0:EVERY, 128:256] = entry_rows([fremote_ref[i] for i in range(4)])
    for r in range(EVERY):
        for half in range(2):
            at = 128 * half
            one = jnp.broadcast_to(rows[r : r + 1, at : at + 128], (E_DEV, 128)) * perm
            lhs[r * E_DEV : (r + 1) * E_DEV, at : at + 128] = one.astype(BF16)
    flux_one = ind_k == ((ind_l & 127) >> 5)
    flux_ind = jnp.concatenate(
        [(flux_one & (ind_l < 128)).astype(BF16), (flux_one & (ind_l >= 128)).astype(BF16)], axis=0
    )
    cf[...] = mdot(lhs[...], flux_ind).reshape(FIELDS, FIELDS, E_DEV, 256)

    low64 = iota((64, 128), 1) < 64
    blocks = []
    for d in range(3):
        padded = jnp.concatenate([stiff_ref[d], jnp.zeros((56, 72), F32)], axis=1)
        blocks.append(jnp.concatenate([twice(padded), jnp.zeros((8, 128), F32)], axis=0))
    for part, block in enumerate((jnp.where(low64, blocks[0], blocks[1]), blocks[2])):
        at = 128 * part
        hi, lo = hi_lo(block)
        vk[0:64, at : at + 128] = hi.astype(BF16)
        vk[64:128, at : at + 128] = hi.astype(BF16)
        vk[128:192, at : at + 128] = lo.astype(BF16)

    for i in range(4):
        sq[32 * i : 32 * i + 21, 0:56] = restrict_ref[i]
    traced = jnp.transpose(twice(sq[...]))
    store_rhs(rt, traced)
    for i in range(4):
        sq[32 * i : 32 * i + 21, 0:56] = lift_ref[i]
    hi, lo = hi_lo(twice(sq[...]))
    lf[0:128, :] = hi.astype(BF16)
    lf[128:256, :] = hi.astype(BF16)
    lf[256:384, :] = lo.astype(BF16)

    sq[...] = jnp.zeros_like(sq)
    for t in range(3):
        sq[21 * t : 21 * t + 21, 0:21] = orient_ref[t]
    turns = jnp.transpose(sq[...])[0:32, :]
    turns = (turns, pltpu.roll(turns, 64, 1))
    none = jnp.zeros((32, 128), F32)
    for nf in range(4):
        wide = [none, none]
        wide[nf // 2] = turns[nf % 2]
        hi, lo = hi_lo(jnp.concatenate(wide, axis=1))
        ob[32 * nf : 32 * nf + 32, :] = hi.astype(BF16)
        ob[128 + 32 * nf : 160 + 32 * nf, :] = hi.astype(BF16)
        ob[256 + 32 * nf : 288 + 32 * nf, :] = lo.astype(BF16)
    hi, lo = hi_lo(traced)
    hi, lo = hi.astype(BF16), lo.astype(BF16)
    store_rhs(qt, mdot(jnp.concatenate([hi, lo, hi], axis=1), ob[...]))

    perm16 = perm[:, 0:16]
    coded = []
    for i in range(4):
        coded.append(perm16 * slot_ref[i : i + 1, :].astype(F32))
    for i in range(4):
        coded.append(perm16 * face_ref[i : i + 1, :].astype(F32))
    for i in range(4):
        coded.append(perm16 * turn_ref[i : i + 1, :].astype(F32))
    coded.append(perm16 * rate_ref[...].astype(F32))
    codes = mdot(jnp.concatenate(coded, axis=0).astype(BF16), jnp.ones((16, 128), BF16))
    codes = codes.astype(jnp.int32)
    slots, faces, turn_of = codes[0:64, 0:64], codes[64:128], codes[128:192]
    fast = codes[192:200, :] == 2
    ghost_slot = 16 + ((elem_lane & 3) ^ 1) * 4 + (elem_lane >> 2)
    target_row = jnp.where((lane16 & 16) > 0, ghost_slot, row)
    def tables(first, count):
        def part(values):
            return jnp.concatenate([values[16 * i + first : 16 * i + first + count] for i in range(4)], axis=0)

        slot_part, face_part, turn_part = part(slots), part(faces), part(turn_of)
        hot = (slot_part == jnp.broadcast_to(target_row[0:1, 0:64], (4 * count, 64))).astype(BF16)
        lane = iota((4 * count, 128), 1)
        inner = lane & 63
        turn_l = (inner >= 21).astype(jnp.int32) + (inner >= 42).astype(jnp.int32)
        mask = ((face_part & 1) == (lane >> 6)) & (turn_part == turn_l)
        return first, count, hot, face_part >= 2, mask.astype(F32)

    place_k = iota((256, 128), 0) & 63
    place_f = place_k - 21 * ((place_k >= 21).astype(jnp.int32) + (place_k >= 42).astype(jnp.int32))
    place_l = iota((256, 128), 1)
    places = [((place_l == place_f + 32 * i) & (place_k < 63)).astype(BF16) for i in range(4)]

    def own_terms(values):
        left = lhs_of(values)
        vol_keep[...] = couple_dirs(mdot(left, vk[...]).reshape(FIELDS, E_DEV, 256), ca, cb, E_DEV)
        own = mdot(left, rt[...]).reshape(FIELDS, E_DEV, 128)
        own_keep[...] = couple(own, lambda c: cf[c, :, :, 0:128])
        hi, lo = hi_lo(mdot(left, qt[...]).reshape(FIELDS, E_DEV, 256))
        zs[:, 0:16, :] = hi.astype(BF16)
        zs[:, 32:48, :] = lo.astype(BF16)

    def ghost_traces(ghosts):
        hi, lo = hi_lo(mdot(lhs_of(ghosts), qt[...]).reshape(FIELDS, E_DEV, 256))
        zs[:, 16:32, :] = hi.astype(BF16)
        zs[:, 48:64, :] = lo.astype(BF16)

    def advanced(table):
        first, count, hot, upper_face, mask = table
        cells = pl.ds(first, count)
        taken = []
        for c in range(FIELDS):
            one = mdot(hot, zs[c])
            taken.append(jnp.where(upper_face, one[:, 128:256], one[:, 0:128]) * mask)
        taken = jnp.stack(taken, axis=0)
        placed = None
        for i in range(4):
            hi, lo = hi_lo(taken[:, count * i : count * i + count, :].reshape(FIELDS * count, 128))
            one = mdot(jnp.concatenate([hi.astype(BF16), lo.astype(BF16)], axis=1), places[i])
            placed = one if placed is None else placed + one
        placed = placed.reshape(FIELDS, count, 128)
        flux = own_keep[:, cells, :] + couple(placed, lambda c: cf[c, :, cells, 128:256])
        hi, lo = hi_lo(flux.reshape(FIELDS * count, 128))
        hi, lo = hi.astype(BF16), lo.astype(BF16)
        lifted = mdot(jnp.concatenate([hi, lo, hi], axis=1), lf[...]).reshape(FIELDS, count, 128)
        return base_keep[:, cells, :] + vol_keep[:, cells, :] - lifted

    fast_rows, slow_rows, all_rows = tables(0, 8), tables(8, 8), tables(0, 16)
    own_terms(early)
    for copy in exchange_a:
        copy.wait()
    odd_row = (row8 & 1) == 1
    by_dom = jnp.where(odd_row, recv_a[0], recv_a[1])
    by_sub = jnp.where(odd_row, recv_a[2], recv_a[3])
    ghost8 = unpack(jnp.where(upper, by_dom, pltpu.roll(by_sub, 2, 1)))
    ghost16 = unpack(jnp.where(upper, pltpu.roll(by_dom, 6, 1), by_sub))
    ghost_traces(jnp.concatenate([ghost8, ghost16], axis=1))
    current = advanced(fast_rows)
    base_keep[:, 0:8, :] = current
    restart = taylor_weight(0.0, 0.5, 0) * current
    for degree in range(1, DERIVS):
        current = derive(current)
        restart = restart + taylor_weight(0.0, 0.5, degree) * current
    late8 = jnp.where(fast[None], restart, late_keep[:, 0:8, :])

    fast_send(pack(late8), send_b)
    exchange_b = copies(lambda p: send_b.at[p // 2], recv_b, 2)
    for copy in exchange_b:
        copy.start()
    base_keep[:, 8:16, :] = advanced(slow_rows)
    own_terms(jnp.concatenate([late8, late_keep[:, 8:16, :]], axis=1))
    for copy in exchange_l:
        copy.wait()
    ghost16 = whole_ghosts(recv_l)
    for copy in exchange_b:
        copy.wait()
    ghost_traces(jnp.concatenate([fast_ghosts(recv_b), ghost16], axis=1))
    final = advanced(all_rows)
    for c in range(FIELDS):
        out_ref[c] = permute(perm_back, final[c])[:, 0:56]


def solution(mesh):
    n_dom, n_sub = mesh.shape["dom"], mesh.shape["sub"]
    cells = (FIELDS, E_DEV, 128)

    def local(
        state,
        stiffness,
        star,
        face_restrict,
        face_lift,
        orient_maps,
        flux_local,
        flux_remote,
        cluster_rate,
        send_list,
        slot,
        face,
        turn,
    ):
        def entries(array):
            return jnp.transpose(array, (1, 2, 0, 3)).reshape(EVERY, array.shape[0], E_DEV)

        table = pltpu.VMEM((4, E_DEV), jnp.int32)
        out = pl.pallas_call(
            lambda *refs: kernel(n_dom, n_sub, *refs),
            out_shape=pltpu.VMEM((FIELDS, E_DEV, MODES), F32),
            in_specs=[pl.BlockSpec(memory_space=pltpu.HBM)] * 13,
            out_specs=pl.BlockSpec(memory_space=pltpu.VMEM),
            scratch_shapes=[
                pltpu.SMEM((1, 4, 4), jnp.int32),
                pltpu.VMEM((FIELDS, E_DEV, MODES), F32),
                pltpu.VMEM((3, MODES, MODES), F32),
                pltpu.VMEM((3, EVERY, E_DEV), F32),
                pltpu.VMEM((4, FACE_MODES, MODES), F32),
                pltpu.VMEM((4, FACE_MODES, MODES), F32),
                pltpu.VMEM((3, FACE_MODES, FACE_MODES), F32),
                pltpu.VMEM((4, EVERY, E_DEV), F32),
                pltpu.VMEM((4, EVERY, E_DEV), F32),
                pltpu.VMEM((1, E_DEV), jnp.int32),
                table,
                table,
                table,
                pltpu.SemaphoreType.DMA((27,)),
                pltpu.VMEM((192, 256), BF16),
                pltpu.VMEM((192, 256), BF16),
                pltpu.VMEM((192, 128), BF16),
                pltpu.VMEM((192, 256), BF16),
                pltpu.VMEM((384, 128), BF16),
                pltpu.VMEM((384, 256), BF16),
                pltpu.VMEM((128, 128), F32),
                pltpu.VMEM((256, 128), F32),
                pltpu.VMEM((88, 256), F32),
                pltpu.VMEM((EVERY * E_DEV, 256), BF16),
                pltpu.VMEM((FIELDS, FIELDS, E_DEV, 128), F32),
                pltpu.VMEM((FIELDS, 5, E_DEV, 128), F32),
                pltpu.VMEM((FIELDS, FIELDS, E_DEV, 256), F32),
                pltpu.VMEM((FIELDS, 64, 256), BF16),
                pltpu.VMEM((DERIVS - 1,) + cells, F32),
                pltpu.VMEM(cells, F32),
                pltpu.VMEM(cells, F32),
                pltpu.VMEM(cells, F32),
                pltpu.VMEM(cells, F32),
                pltpu.VMEM((2, 5, 8, 128), F32),
                pltpu.VMEM((5, 8, 128), F32),
                pltpu.VMEM((2, 3, 8, 128), F32),
                pltpu.VMEM((4, 5, 8, 128), F32),
                pltpu.VMEM((4, 5, 8, 128), F32),
                pltpu.VMEM((4, 3, 8, 128), F32),
                pltpu.SemaphoreType.DMA((3, 4)),
                pltpu.SemaphoreType.DMA((3, 4)),
            ],
            compiler_params=pltpu.CompilerParams(
                collective_id=0, has_side_effects=True
            ),
            name="ader_step",
        )(
            send_list,
            jnp.transpose(state, (1, 2, 0)),
            stiffness,
            entries(star),
            jnp.transpose(face_restrict, (1, 0, 2)),
            jnp.transpose(face_lift, (2, 0, 1)),
            orient_maps,
            entries(flux_local),
            entries(flux_remote),
            cluster_rate.reshape(1, E_DEV),
            slot,
            face,
            turn,
        )
        return jnp.transpose(out, (2, 0, 1))

    along = ("dom", "sub")
    placed = (
        P(None, None, along),
        P(),
        P(None, None, None, along),
        P(),
        P(),
        P(),
        P(None, None, None, along),
        P(None, None, None, along),
        P(along),
        P(along, None, None),
        P(None, along),
        P(None, along),
        P(None, along),
    )
    return jax.shard_map(
        local, mesh=mesh, in_specs=placed, out_specs=P(None, None, along), check_vma=False
    )
```

```python
import math

import jax
import jax.numpy as jnp
from jax import lax
from jax.experimental import pallas as pl
from jax.experimental.pallas import tpu as pltpu
from jax.sharding import PartitionSpec as P

MODES = 56
FACE_MODES = 21
FIELDS = 9
DERIVS = 6
E_DEV = 16
EVERY = FIELDS * FIELDS
MESH = pl.DeviceIdType.MESH
F32 = jnp.float32
BF16 = jnp.bfloat16


def taylor_weight(lower, upper, degree):
    return (upper ** (degree + 1) - lower ** (degree + 1)) / math.factorial(degree + 1)


def iota(shape, axis):
    return lax.broadcasted_iota(jnp.int32, shape, axis)


def hi_lo(x):
    hi = x.astype(BF16).astype(F32)
    return hi, x - hi


def mdot(a, b):
    return jnp.dot(a, b, preferred_element_type=F32)


def twice(x):
    return x + pltpu.roll(x, 64, 1)


def lhs_of(values):
    hi, lo = hi_lo(values)
    low_half = iota(values.shape, 2) < 64
    one = jnp.where(low_half, hi, lo).reshape(values.shape[0] * values.shape[1], 128).astype(BF16)
    return jnp.concatenate([one, one[:, 0:64]], axis=1)


def store_rhs(target, value):
    hi, lo = hi_lo(value)
    target[0:128, :] = hi.astype(BF16)
    target[128:192, :] = lo[0:64].astype(BF16)


def couple(values, coefs):
    result = values[0][None] * coefs(0)
    for c in range(1, FIELDS):
        result = result + values[c][None] * coefs(c)
    return result


def couple_dirs(product, ca, cb, count):
    pair = couple(product[:, :, 0:128], lambda c: ca[c, :, 0:count, :])
    third = couple(product[:, :, 128:256], lambda c: cb[c, :, 0:count, :])
    swapped = pltpu.roll(third, 64, 2)
    low_half = iota(third.shape, 2) < 64
    even = jnp.where(low_half, third, swapped)
    odd = jnp.where(low_half, swapped, third)
    spread_third = jnp.stack([(even, odd)[j % 2][j // 2] for j in range(FIELDS)], axis=0)
    return pair + pltpu.roll(pair, 64, 2) + spread_third


def kernel(n_dom, n_sub, *refs):
    (
        send_hbm,
        sol_hbm,
        stiff_hbm,
        star_hbm,
        restrict_hbm,
        lift_hbm,
        orient_hbm,
        flocal_hbm,
        fremote_hbm,
        rate_hbm,
        slot_hbm,
        face_hbm,
        turn_hbm,
        out_ref,
        send_ref,
        sol_ref,
        stiff_ref,
        star_ref,
        restrict_ref,
        lift_ref,
        orient_ref,
        flocal_ref,
        fremote_ref,
        rate_ref,
        slot_ref,
        face_ref,
        turn_ref,
        in_sem,
        dk,
        vk,
        rt,
        qt,
        lf,
        ob,
        sq,
        tall,
        rows,
        lhs,
        ca,
        cb,
        cf,
        zs,
        deriv_keep,
        codes_keep,
        places,
        late_keep,
        base_keep,
        own_keep,
        vol_keep,
        send_a,
        send_l,
        send_b,
        recv_a,
        recv_l,
        recv_b,
        ssem,
        rsem,
    ) = refs
    dom = lax.axis_index("dom")
    sub = lax.axis_index("sub")
    peers = (
        (lax.rem(dom + n_dom - 1, n_dom), sub),
        (lax.rem(dom + 1, n_dom), sub),
        (dom, lax.rem(sub + n_sub - 1, n_sub)),
        (dom, lax.rem(sub + 1, n_sub)),
    )

    moves = [(send_hbm, send_ref), (sol_hbm, sol_ref), (stiff_hbm, stiff_ref)]
    moves += [(star_hbm.at[:, d, :], star_ref.at[d]) for d in range(3)]
    first_part = len(moves)
    moves += [(flocal_hbm.at[:, i, :], flocal_ref.at[i]) for i in range(4)]
    moves += [(fremote_hbm.at[:, i, :], fremote_ref.at[i]) for i in range(4)]
    moves += [(restrict_hbm.at[:, i, :], restrict_ref.at[i]) for i in range(4)]
    moves += [(lift_hbm.at[:, i, :], lift_ref.at[i]) for i in range(4)]
    moves += [(orient_hbm, orient_ref), (rate_hbm, rate_ref), (slot_hbm, slot_ref)]
    moves += [(face_hbm, face_ref), (turn_hbm, turn_ref)]
    loads = [
        pltpu.make_async_copy(source, target, in_sem.at[n])
        for n, (source, target) in enumerate(moves)
    ]
    for load in loads:
        load.start()

    barrier = pltpu.get_barrier_semaphore()
    for peer in peers:
        pl.semaphore_signal(barrier, inc=1, device_id=peer, device_id_type=MESH)

    def copies(source, target, which):
        return [
            pltpu.make_async_remote_copy(
                src_ref=source(p),
                dst_ref=target.at[p ^ 1],
                send_sem=ssem.at[which, p],
                recv_sem=rsem.at[which, p ^ 1],
                device_id=peers[p],
                device_id_type=MESH,
            )
            for p in range(4)
        ]

    lane16 = iota((E_DEV, 128), 1)
    sub16 = iota((E_DEV, 128), 0)
    elem_lane = lane16 & 15
    ind_k = (iota((128, 256), 0) >> 4) & 3
    ind_l = iota((128, 256), 1)
    star_ind = (ind_k == jnp.where(ind_l < 128, ind_l >> 6, 2)).astype(BF16)
    tall[...] = jnp.zeros_like(tall)
    sq[...] = jnp.zeros_like(sq)
    rows[...] = jnp.zeros_like(rows)

    for load in loads[0:first_part]:
        load.wait()

    column = jnp.zeros((E_DEV, 128), jnp.int32)
    row = jnp.zeros((E_DEV, 128), jnp.int32)
    for e in range(E_DEV):
        value = send_ref[0, e % 4, e // 4]
        column = jnp.where(sub16 == e, value, column)
        row = jnp.where(elem_lane == e, value, row)
    perm = (column == elem_lane).astype(F32)
    perm_back = (sub16 == row).astype(F32)

    def permute(matrix, values):
        hi, lo = hi_lo(values)
        stacked = jnp.concatenate([hi, lo], axis=0).astype(BF16)
        return mdot(matrix[:, 0:32].astype(BF16), stacked)

    def entry_rows(parts):
        empty = [jnp.zeros((EVERY, 16), F32)] * (4 - len(parts))
        hi, lo = hi_lo(jnp.concatenate(parts + empty, axis=1))
        return jnp.concatenate([hi, lo], axis=1)

    rows[0:EVERY, 0:128] = entry_rows([star_ref[d] for d in range(3)])
    for r in range(EVERY):
        one = jnp.broadcast_to(rows[r : r + 1, 0:128], (E_DEV, 128)) * perm
        lhs[r * E_DEV : (r + 1) * E_DEV, 0:128] = one.astype(BF16)
    product = mdot(lhs[:, 0:128], star_ind).reshape(FIELDS, FIELDS, E_DEV, 256)
    ca[...] = product[:, :, :, 0:128]
    low_cell = lane16 < 64
    for j in range(0, FIELDS, 2):
        one = product[:, j, :, 128:256]
        if j + 1 < FIELDS:
            one = jnp.where(low_cell[None], one, product[:, j + 1, :, 128:256])
        cb[:, j // 2] = one

    for d, at in ((0, 0), (1, 64), (2, 128), (2, 192)):
        tall[at : at + 56, 0:56] = -stiff_ref[d]
    for half in range(2):
        at = 128 * half
        block = jnp.transpose(twice(tall[at : at + 128, :]))
        hi, lo = hi_lo(block)
        dk[0:128, at : at + 128] = hi.astype(BF16)
        dk[128:192, at : at + 128] = lo[0:64].astype(BF16)

    state = []
    for c in range(FIELDS):
        one = jnp.concatenate([sol_ref[c], jnp.zeros((E_DEV, 72), F32)], axis=1)
        state.append(permute(perm, twice(one)))
    state = jnp.stack(state, axis=0)
    base_keep[...] = state

    def derive(values):
        count = values.shape[1]
        product = mdot(lhs_of(values), dk[...]).reshape(FIELDS, count, 256)
        return couple_dirs(product, ca, cb, count)

    current = state
    early = taylor_weight(0.0, 0.5, 0) * current
    for degree in range(1, DERIVS):
        current = derive(current)
        early = early + taylor_weight(0.0, 0.5, degree) * current
        deriv_keep[degree - 1] = current

    row8 = iota((5, 8, 128), 1)
    low8 = iota((5, 8, 128), 2) < 64

    def pack(values):
        return jnp.stack(
            [values[8] if q == 4 else jnp.where(low8[0], values[2 * q], values[2 * q + 1]) for q in range(5)],
            axis=0,
        )

    def unpack(values):
        other = pltpu.roll(values, 64, 2)
        even = jnp.where(low8, values, other)
        odd = jnp.where(low8, other, values)
        return jnp.stack([(even, odd)[c % 2][c // 2] for c in range(FIELDS)], axis=0)

    def whole_ghosts(source):
        side = row8 & 3
        one = jnp.where(side == 0, source[1], source[0])
        two = jnp.where(side == 2, source[3], source[2])
        return unpack(jnp.where(side < 2, one, two))

    upper3 = (iota((3, 8, 128), 1) & 2) == 0
    odd3 = (iota((3, 8, 128), 1) & 1) == 1

    def fast_send(values, target):
        even = jnp.stack([values[0], values[2], values[4]], axis=0)
        odd = jnp.stack([values[1], values[3], values[4]], axis=0)
        target[0] = jnp.where(upper3, even, pltpu.roll(odd, 2, 1))
        target[1] = jnp.where(upper3, pltpu.roll(even, 6, 1), odd)

    def fast_ghosts(source):
        by_dom = jnp.where(odd3, source[0], source[1])
        by_sub = jnp.where(odd3, source[2], source[3])
        even = jnp.where(upper3, by_dom, pltpu.roll(by_sub, 2, 1))
        odd = jnp.where(upper3, pltpu.roll(by_dom, 6, 1), by_sub)
        return unpack(jnp.stack([even[0], odd[0], even[1], odd[1], even[2]], axis=0))

    first8, last8 = pack(early[:, 0:8, :]), pack(early[:, 8:16, :])
    upper = (row8 & 2) == 0
    send_a[0] = jnp.where(upper, first8, pltpu.roll(last8, 2, 1))
    send_a[1] = jnp.where(upper, pltpu.roll(first8, 6, 1), last8)
    pl.semaphore_wait(barrier, 4)
    exchange_a = copies(lambda p: send_a.at[p // 2], recv_a, 0)
    for copy in exchange_a:
        copy.start()

    @pl.when(dom < n_dom)
    def _():
        late = taylor_weight(0.5, 1.0, 0) * base_keep[...]
        for degree in range(1, DERIVS):
            late = late + taylor_weight(0.5, 1.0, degree) * deriv_keep[degree - 1]
        late_keep[...] = late
        send_l[...] = pack(late[:, 8:16, :])

    exchange_l = copies(lambda p: send_l, recv_l, 1)
    for copy in exchange_l:
        copy.start()

    for load in loads[first_part:]:
        load.wait()
    @pl.when(dom < n_dom)
    def _():
        rows[0:EVERY, 0:128] = entry_rows([flocal_ref[i] for i in range(4)])
        rows[0:EVERY, 128:256] = entry_rows([fremote_ref[i] for i in range(4)])
        for r in range(EVERY):
            for half in range(2):
                at = 128 * half
                one = jnp.broadcast_to(rows[r : r + 1, at : at + 128], (E_DEV, 128)) * perm
                lhs[r * E_DEV : (r + 1) * E_DEV, at : at + 128] = one.astype(BF16)
        flux_one = ind_k == ((ind_l & 127) >> 5)
        flux_ind = jnp.concatenate(
            [(flux_one & (ind_l < 128)).astype(BF16), (flux_one & (ind_l >= 128)).astype(BF16)], axis=0
        )
        cf[...] = mdot(lhs[...], flux_ind).reshape(FIELDS, FIELDS, E_DEV, 256)

        low64 = iota((64, 128), 1) < 64
        blocks = []
        for d in range(3):
            padded = jnp.concatenate([stiff_ref[d], jnp.zeros((56, 72), F32)], axis=1)
            blocks.append(jnp.concatenate([twice(padded), jnp.zeros((8, 128), F32)], axis=0))
        for part, block in enumerate((jnp.where(low64, blocks[0], blocks[1]), blocks[2])):
            at = 128 * part
            hi, lo = hi_lo(block)
            vk[0:64, at : at + 128] = hi.astype(BF16)
            vk[64:128, at : at + 128] = hi.astype(BF16)
            vk[128:192, at : at + 128] = lo.astype(BF16)

        for i in range(4):
            sq[32 * i : 32 * i + 21, 0:56] = restrict_ref[i]
        traced = jnp.transpose(twice(sq[...]))
        store_rhs(rt, traced)
        for i in range(4):
            sq[32 * i : 32 * i + 21, 0:56] = lift_ref[i]
        hi, lo = hi_lo(twice(sq[...]))
        lf[0:128, :] = hi.astype(BF16)
        lf[128:256, :] = hi.astype(BF16)
        lf[256:384, :] = lo.astype(BF16)

        sq[...] = jnp.zeros_like(sq)
        for t in range(3):
            sq[21 * t : 21 * t + 21, 0:21] = orient_ref[t]
        turns = jnp.transpose(sq[...])[0:32, :]
        turns = (turns, pltpu.roll(turns, 64, 1))
        none = jnp.zeros((32, 128), F32)
        for nf in range(4):
            wide = [none, none]
            wide[nf // 2] = turns[nf % 2]
            hi, lo = hi_lo(jnp.concatenate(wide, axis=1))
            ob[32 * nf : 32 * nf + 32, :] = hi.astype(BF16)
            ob[128 + 32 * nf : 160 + 32 * nf, :] = hi.astype(BF16)
            ob[256 + 32 * nf : 288 + 32 * nf, :] = lo.astype(BF16)
        hi, lo = hi_lo(traced)
        hi, lo = hi.astype(BF16), lo.astype(BF16)
        store_rhs(qt, mdot(jnp.concatenate([hi, lo, hi], axis=1), ob[...]))

        perm16 = perm[:, 0:16]
        coded = []
        for i in range(4):
            coded.append(perm16 * slot_ref[i : i + 1, :].astype(F32))
        for i in range(4):
            coded.append(perm16 * face_ref[i : i + 1, :].astype(F32))
        for i in range(4):
            coded.append(perm16 * turn_ref[i : i + 1, :].astype(F32))
        coded.append(perm16 * rate_ref[...].astype(F32))
        codes_keep[...] = mdot(jnp.concatenate(coded, axis=0).astype(BF16), jnp.ones((16, 128), BF16))
        place_k = iota((256, 128), 0) & 63
        place_f = place_k - 21 * ((place_k >= 21).astype(jnp.int32) + (place_k >= 42).astype(jnp.int32))
        place_l = iota((256, 128), 1)
        for i in range(4):
            places[i] = ((place_l == place_f + 32 * i) & (place_k < 63)).astype(BF16)

    codes = codes_keep[...].astype(jnp.int32)
    slots, faces, turn_of = codes[0:64, 0:64], codes[64:128], codes[128:192]
    fast = codes[192:200, :] == 2
    ghost_slot = 16 + ((elem_lane & 3) ^ 1) * 4 + (elem_lane >> 2)
    target_row = jnp.where((lane16 & 16) > 0, ghost_slot, row)
    def tables(first, count):
        def part(values):
            return jnp.concatenate([values[16 * i + first : 16 * i + first + count] for i in range(4)], axis=0)

        slot_part, face_part, turn_part = part(slots), part(faces), part(turn_of)
        hot = (slot_part == jnp.broadcast_to(target_row[0:1, 0:64], (4 * count, 64))).astype(BF16)
        lane = iota((4 * count, 128), 1)
        inner = lane & 63
        turn_l = (inner >= 21).astype(jnp.int32) + (inner >= 42).astype(jnp.int32)
        mask = ((face_part & 1) == (lane >> 6)) & (turn_part == turn_l)
        return first, count, hot, face_part >= 2, mask.astype(F32)

    def own_terms(values):
        left = lhs_of(values)
        vol_keep[...] = couple_dirs(mdot(left, vk[...]).reshape(FIELDS, E_DEV, 256), ca, cb, E_DEV)
        own = mdot(left, rt[...]).reshape(FIELDS, E_DEV, 128)
        own_keep[...] = couple(own, lambda c: cf[c, :, :, 0:128])
        hi, lo = hi_lo(mdot(left, qt[...]).reshape(FIELDS, E_DEV, 256))
        zs[:, 0:16, :] = hi.astype(BF16)
        zs[:, 32:48, :] = lo.astype(BF16)

    def ghost_traces(ghosts):
        hi, lo = hi_lo(mdot(lhs_of(ghosts), qt[...]).reshape(FIELDS, E_DEV, 256))
        zs[:, 16:32, :] = hi.astype(BF16)
        zs[:, 48:64, :] = lo.astype(BF16)

    def advanced(table):
        first, count, hot, upper_face, mask = table
        cells = pl.ds(first, count)
        taken = []
        for c in range(FIELDS):
            one = mdot(hot, zs[c])
            taken.append(jnp.where(upper_face, one[:, 128:256], one[:, 0:128]) * mask)
        taken = jnp.stack(taken, axis=0)
        placed = None
        for i in range(4):
            hi, lo = hi_lo(taken[:, count * i : count * i + count, :].reshape(FIELDS * count, 128))
            one = mdot(jnp.concatenate([hi.astype(BF16), lo.astype(BF16)], axis=1), places[i])
            placed = one if placed is None else placed + one
        placed = placed.reshape(FIELDS, count, 128)
        flux = own_keep[:, cells, :] + couple(placed, lambda c: cf[c, :, cells, 128:256])
        hi, lo = hi_lo(flux.reshape(FIELDS * count, 128))
        hi, lo = hi.astype(BF16), lo.astype(BF16)
        lifted = mdot(jnp.concatenate([hi, lo, hi], axis=1), lf[...]).reshape(FIELDS, count, 128)
        return base_keep[:, cells, :] + vol_keep[:, cells, :] - lifted

    fast_rows, slow_rows, all_rows = tables(0, 8), tables(8, 8), tables(0, 16)
    own_terms(early)
    for copy in exchange_a:
        copy.wait()
    odd_row = (row8 & 1) == 1
    by_dom = jnp.where(odd_row, recv_a[0], recv_a[1])
    by_sub = jnp.where(odd_row, recv_a[2], recv_a[3])
    ghost8 = unpack(jnp.where(upper, by_dom, pltpu.roll(by_sub, 2, 1)))
    ghost16 = unpack(jnp.where(upper, pltpu.roll(by_dom, 6, 1), by_sub))
    ghost_traces(jnp.concatenate([ghost8, ghost16], axis=1))
    current = advanced(fast_rows)
    base_keep[:, 0:8, :] = current
    restart = taylor_weight(0.0, 0.5, 0) * current
    for degree in range(1, DERIVS):
        current = derive(current)
        restart = restart + taylor_weight(0.0, 0.5, degree) * current
    late8 = jnp.where(fast[None], restart, late_keep[:, 0:8, :])

    fast_send(pack(late8), send_b)
    exchange_b = copies(lambda p: send_b.at[p // 2], recv_b, 2)
    for copy in exchange_b:
        copy.start()

    @pl.when(dom < n_dom)
    def _():
        base_keep[:, 8:16, :] = advanced(slow_rows)
        own_terms(jnp.concatenate([late8, late_keep[:, 8:16, :]], axis=1))

    for copy in exchange_l:
        copy.wait()
    ghost16 = whole_ghosts(recv_l)
    for copy in exchange_b:
        copy.wait()
    ghost_traces(jnp.concatenate([fast_ghosts(recv_b), ghost16], axis=1))
    final = advanced(all_rows)
    for c in range(FIELDS):
        out_ref[c] = permute(perm_back, final[c])[:, 0:56]


def solution(mesh):
    n_dom, n_sub = mesh.shape["dom"], mesh.shape["sub"]
    cells = (FIELDS, E_DEV, 128)

    def local(
        state,
        stiffness,
        star,
        face_restrict,
        face_lift,
        orient_maps,
        flux_local,
        flux_remote,
        cluster_rate,
        send_list,
        slot,
        face,
        turn,
    ):
        def entries(array):
            return jnp.transpose(array, (1, 2, 0, 3)).reshape(EVERY, array.shape[0], E_DEV)

        table = pltpu.VMEM((4, E_DEV), jnp.int32)
        out = pl.pallas_call(
            lambda *refs: kernel(n_dom, n_sub, *refs),
            out_shape=pltpu.VMEM((FIELDS, E_DEV, MODES), F32),
            in_specs=[pl.BlockSpec(memory_space=pltpu.HBM)] * 13,
            out_specs=pl.BlockSpec(memory_space=pltpu.VMEM),
            scratch_shapes=[
                pltpu.SMEM((1, 4, 4), jnp.int32),
                pltpu.VMEM((FIELDS, E_DEV, MODES), F32),
                pltpu.VMEM((3, MODES, MODES), F32),
                pltpu.VMEM((3, EVERY, E_DEV), F32),
                pltpu.VMEM((4, FACE_MODES, MODES), F32),
                pltpu.VMEM((4, FACE_MODES, MODES), F32),
                pltpu.VMEM((3, FACE_MODES, FACE_MODES), F32),
                pltpu.VMEM((4, EVERY, E_DEV), F32),
                pltpu.VMEM((4, EVERY, E_DEV), F32),
                pltpu.VMEM((1, E_DEV), jnp.int32),
                table,
                table,
                table,
                pltpu.SemaphoreType.DMA((27,)),
                pltpu.VMEM((192, 256), BF16),
                pltpu.VMEM((192, 256), BF16),
                pltpu.VMEM((192, 128), BF16),
                pltpu.VMEM((192, 256), BF16),
                pltpu.VMEM((384, 128), BF16),
                pltpu.VMEM((384, 256), BF16),
                pltpu.VMEM((128, 128), F32),
                pltpu.VMEM((256, 128), F32),
                pltpu.VMEM((88, 256), F32),
                pltpu.VMEM((EVERY * E_DEV, 256), BF16),
                pltpu.VMEM((FIELDS, FIELDS, E_DEV, 128), F32),
                pltpu.VMEM((FIELDS, 5, E_DEV, 128), F32),
                pltpu.VMEM((FIELDS, FIELDS, E_DEV, 256), F32),
                pltpu.VMEM((FIELDS, 64, 256), BF16),
                pltpu.VMEM((DERIVS - 1,) + cells, F32),
                pltpu.VMEM((208, 128), F32),
                pltpu.VMEM((4, 256, 128), BF16),
                pltpu.VMEM(cells, F32),
                pltpu.VMEM(cells, F32),
                pltpu.VMEM(cells, F32),
                pltpu.VMEM(cells, F32),
                pltpu.VMEM((2, 5, 8, 128), F32),
                pltpu.VMEM((5, 8, 128), F32),
                pltpu.VMEM((2, 3, 8, 128), F32),
                pltpu.VMEM((4, 5, 8, 128), F32),
                pltpu.VMEM((4, 5, 8, 128), F32),
                pltpu.VMEM((4, 3, 8, 128), F32),
                pltpu.SemaphoreType.DMA((3, 4)),
                pltpu.SemaphoreType.DMA((3, 4)),
            ],
            compiler_params=pltpu.CompilerParams(
                collective_id=0, has_side_effects=True
            ),
            name="ader_step",
        )(
            send_list,
            jnp.transpose(state, (1, 2, 0)),
            stiffness,
            entries(star),
            jnp.transpose(face_restrict, (1, 0, 2)),
            jnp.transpose(face_lift, (2, 0, 1)),
            orient_maps,
            entries(flux_local),
            entries(flux_remote),
            cluster_rate.reshape(1, E_DEV),
            slot,
            face,
            turn,
        )
        return jnp.transpose(out, (2, 0, 1))

    along = ("dom", "sub")
    placed = (
        P(None, None, along),
        P(),
        P(None, None, None, along),
        P(),
        P(),
        P(),
        P(None, None, None, along),
        P(None, None, None, along),
        P(along),
        P(along, None, None),
        P(None, along),
        P(None, along),
        P(None, along),
    )
    return jax.shard_map(
        local, mesh=mesh, in_specs=placed, out_specs=P(None, None, along), check_vma=False
    )
```

```python
import math

import jax
import jax.numpy as jnp
from jax import lax
from jax.experimental import pallas as pl
from jax.experimental.pallas import tpu as pltpu
from jax.sharding import PartitionSpec as P

MODES = 56
FACE_MODES = 21
FIELDS = 9
DERIVS = 6
E_DEV = 16
EVERY = FIELDS * FIELDS
MESH = pl.DeviceIdType.MESH
F32 = jnp.float32
BF16 = jnp.bfloat16


def taylor_weight(lower, upper, degree):
    return (upper ** (degree + 1) - lower ** (degree + 1)) / math.factorial(degree + 1)


def iota(shape, axis):
    return lax.broadcasted_iota(jnp.int32, shape, axis)


def hi_lo(x):
    hi = x.astype(BF16).astype(F32)
    return hi, x - hi


def mdot(a, b):
    return jnp.dot(a, b, preferred_element_type=F32)


def twice(x):
    return x + pltpu.roll(x, 64, 1)


def lhs_of(values):
    hi, lo = hi_lo(values)
    low_half = iota(values.shape, 2) < 64
    one = jnp.where(low_half, hi, lo).reshape(values.shape[0] * values.shape[1], 128).astype(BF16)
    return jnp.concatenate([one, one[:, 0:64]], axis=1)


def store_rhs(target, value):
    hi, lo = hi_lo(value)
    target[0:128, :] = hi.astype(BF16)
    target[128:192, :] = lo[0:64].astype(BF16)


def couple(values, coefs):
    result = values[0][None] * coefs(0)
    for c in range(1, FIELDS):
        result = result + values[c][None] * coefs(c)
    return result


def couple_dirs(product, ca, cb, count):
    pair = couple(product[:, :, 0:128], lambda c: ca[c, :, 0:count, :])
    third = couple(product[:, :, 128:256], lambda c: cb[c, :, 0:count, :])
    swapped = pltpu.roll(third, 64, 2)
    low_half = iota(third.shape, 2) < 64
    even = jnp.where(low_half, third, swapped)
    odd = jnp.where(low_half, swapped, third)
    spread_third = jnp.stack([(even, odd)[j % 2][j // 2] for j in range(FIELDS)], axis=0)
    return pair + pltpu.roll(pair, 64, 2) + spread_third


def kernel(n_dom, n_sub, *refs):
    (
        send_hbm,
        sol_hbm,
        stiff_hbm,
        star_hbm,
        restrict_hbm,
        lift_hbm,
        orient_hbm,
        flocal_hbm,
        fremote_hbm,
        rate_hbm,
        slot_hbm,
        face_hbm,
        turn_hbm,
        out_ref,
        send_ref,
        sol_ref,
        stiff_ref,
        star_ref,
        restrict_ref,
        lift_ref,
        orient_ref,
        flocal_ref,
        fremote_ref,
        rate_ref,
        slot_ref,
        face_ref,
        turn_ref,
        in_sem,
        dk,
        vk,
        rt,
        qt,
        lf,
        ob,
        sq,
        tall,
        rows,
        lhs,
        ca,
        cb,
        cf,
        zs,
        deriv_keep,
        codes_keep,
        places,
        late_keep,
        base_keep,
        own_keep,
        vol_keep,
        send_a,
        send_l,
        send_b,
        recv_a,
        recv_l,
        recv_b,
        ssem,
        rsem,
    ) = refs
    dom = lax.axis_index("dom")
    sub = lax.axis_index("sub")
    peers = (
        (lax.rem(dom + n_dom - 1, n_dom), sub),
        (lax.rem(dom + 1, n_dom), sub),
        (dom, lax.rem(sub + n_sub - 1, n_sub)),
        (dom, lax.rem(sub + 1, n_sub)),
    )

    moves = [(send_hbm, send_ref), (sol_hbm, sol_ref), (stiff_hbm, stiff_ref)]
    moves += [(star_hbm.at[:, d, :], star_ref.at[d]) for d in range(3)]
    first_part = len(moves)
    moves += [(flocal_hbm.at[:, i, :], flocal_ref.at[i]) for i in range(4)]
    moves += [(fremote_hbm.at[:, i, :], fremote_ref.at[i]) for i in range(4)]
    moves += [(restrict_hbm.at[:, i, :], restrict_ref.at[i]) for i in range(4)]
    moves += [(lift_hbm.at[:, i, :], lift_ref.at[i]) for i in range(4)]
    moves += [(orient_hbm, orient_ref), (rate_hbm, rate_ref), (slot_hbm, slot_ref)]
    moves += [(face_hbm, face_ref), (turn_hbm, turn_ref)]
    loads = [
        pltpu.make_async_copy(source, target, in_sem.at[n])
        for n, (source, target) in enumerate(moves)
    ]
    for load in loads:
        load.start()

    barrier = pltpu.get_barrier_semaphore()
    for peer in peers:
        pl.semaphore_signal(barrier, inc=1, device_id=peer, device_id_type=MESH)

    def copies(source, target, which):
        return [
            pltpu.make_async_remote_copy(
                src_ref=source(p),
                dst_ref=target.at[p ^ 1],
                send_sem=ssem.at[which, p],
                recv_sem=rsem.at[which, p ^ 1],
                device_id=peers[p],
                device_id_type=MESH,
            )
            for p in range(4)
        ]

    lane16 = iota((E_DEV, 128), 1)
    sub16 = iota((E_DEV, 128), 0)
    elem_lane = lane16 & 15
    ind_k = (iota((128, 256), 0) >> 4) & 3
    ind_l = iota((128, 256), 1)
    star_ind = (ind_k == jnp.where(ind_l < 128, ind_l >> 6, 2)).astype(BF16)
    tall[...] = jnp.zeros_like(tall)
    sq[...] = jnp.zeros_like(sq)
    rows[...] = jnp.zeros_like(rows)

    for load in loads[0:first_part]:
        load.wait()

    column = jnp.zeros((E_DEV, 128), jnp.int32)
    row = jnp.zeros((E_DEV, 128), jnp.int32)
    for e in range(E_DEV):
        value = send_ref[0, e % 4, e // 4]
        column = jnp.where(sub16 == e, value, column)
        row = jnp.where(elem_lane == e, value, row)
    perm = (column == elem_lane).astype(F32)
    perm_back = (sub16 == row).astype(F32)

    def permute(matrix, values):
        hi, lo = hi_lo(values)
        stacked = jnp.concatenate([hi, lo], axis=0).astype(BF16)
        return mdot(matrix[:, 0:32].astype(BF16), stacked)

    def entry_rows(parts):
        empty = [jnp.zeros((EVERY, 16), F32)] * (4 - len(parts))
        hi, lo = hi_lo(jnp.concatenate(parts + empty, axis=1))
        return jnp.concatenate([hi, lo], axis=1)

    rows[0:EVERY, 0:128] = entry_rows([star_ref[d] for d in range(3)])
    for r in range(EVERY):
        one = jnp.broadcast_to(rows[r : r + 1, 0:128], (E_DEV, 128)) * perm
        lhs[r * E_DEV : (r + 1) * E_DEV, 0:128] = one.astype(BF16)
    product = mdot(lhs[:, 0:128], star_ind).reshape(FIELDS, FIELDS, E_DEV, 256)
    ca[...] = product[:, :, :, 0:128]
    low_cell = lane16 < 64
    for j in range(0, FIELDS, 2):
        one = product[:, j, :, 128:256]
        if j + 1 < FIELDS:
            one = jnp.where(low_cell[None], one, product[:, j + 1, :, 128:256])
        cb[:, j // 2] = one

    for d, at in ((0, 0), (1, 64), (2, 128), (2, 192)):
        tall[at : at + 56, 0:56] = -stiff_ref[d]
    for half in range(2):
        at = 128 * half
        block = jnp.transpose(twice(tall[at : at + 128, :]))
        hi, lo = hi_lo(block)
        dk[0:128, at : at + 128] = hi.astype(BF16)
        dk[128:192, at : at + 128] = lo[0:64].astype(BF16)

    state = []
    for c in range(FIELDS):
        one = jnp.concatenate([sol_ref[c], jnp.zeros((E_DEV, 72), F32)], axis=1)
        state.append(permute(perm, twice(one)))
    state = jnp.stack(state, axis=0)
    base_keep[...] = state

    def derive(values):
        count = values.shape[1]
        product = mdot(lhs_of(values), dk[...]).reshape(FIELDS, count, 256)
        return couple_dirs(product, ca, cb, count)

    current = state
    early = taylor_weight(0.0, 0.5, 0) * current
    for degree in range(1, DERIVS):
        current = derive(current)
        early = early + taylor_weight(0.0, 0.5, degree) * current
        deriv_keep[degree - 1] = current

    row8 = iota((5, 8, 128), 1)
    low8 = iota((5, 8, 128), 2) < 64

    def pack(values):
        return jnp.stack(
            [values[8] if q == 4 else jnp.where(low8[0], values[2 * q], values[2 * q + 1]) for q in range(5)],
            axis=0,
        )

    def unpack(values):
        other = pltpu.roll(values, 64, 2)
        even = jnp.where(low8, values, other)
        odd = jnp.where(low8, other, values)
        return jnp.stack([(even, odd)[c % 2][c // 2] for c in range(FIELDS)], axis=0)

    def whole_ghosts(source):
        side = row8 & 3
        one = jnp.where(side == 0, source[1], source[0])
        two = jnp.where(side == 2, source[3], source[2])
        return unpack(jnp.where(side < 2, one, two))

    upper3 = (iota((3, 8, 128), 1) & 2) == 0
    odd3 = (iota((3, 8, 128), 1) & 1) == 1

    def fast_send(values, target):
        even = jnp.stack([values[0], values[2], values[4]], axis=0)
        odd = jnp.stack([values[1], values[3], values[4]], axis=0)
        target[0] = jnp.where(upper3, even, pltpu.roll(odd, 2, 1))
        target[1] = jnp.where(upper3, pltpu.roll(even, 6, 1), odd)

    def fast_ghosts(source):
        by_dom = jnp.where(odd3, source[0], source[1])
        by_sub = jnp.where(odd3, source[2], source[3])
        even = jnp.where(upper3, by_dom, pltpu.roll(by_sub, 2, 1))
        odd = jnp.where(upper3, pltpu.roll(by_dom, 6, 1), by_sub)
        return unpack(jnp.stack([even[0], odd[0], even[1], odd[1], even[2]], axis=0))

    first8, last8 = pack(early[:, 0:8, :]), pack(early[:, 8:16, :])
    upper = (row8 & 2) == 0
    send_a[0] = jnp.where(upper, first8, pltpu.roll(last8, 2, 1))
    send_a[1] = jnp.where(upper, pltpu.roll(first8, 6, 1), last8)
    pl.semaphore_wait(barrier, 4)
    exchange_a = copies(lambda p: send_a.at[p // 2], recv_a, 0)
    for copy in exchange_a:
        copy.start()

    @pl.when(dom < n_dom)
    def _():
        late = taylor_weight(0.5, 1.0, 0) * base_keep[...]
        for degree in range(1, DERIVS):
            late = late + taylor_weight(0.5, 1.0, degree) * deriv_keep[degree - 1]
        late_keep[...] = late
        send_l[...] = pack(late[:, 8:16, :])

    exchange_l = copies(lambda p: send_l, recv_l, 1)
    for copy in exchange_l:
        copy.start()

    for load in loads[first_part:]:
        load.wait()
    @pl.when(dom < n_dom)
    def _():
        rows[0:EVERY, 0:128] = entry_rows([flocal_ref[i] for i in range(4)])
        rows[0:EVERY, 128:256] = entry_rows([fremote_ref[i] for i in range(4)])
        for r in range(EVERY):
            for half in range(2):
                at = 128 * half
                one = jnp.broadcast_to(rows[r : r + 1, at : at + 128], (E_DEV, 128)) * perm
                lhs[r * E_DEV : (r + 1) * E_DEV, at : at + 128] = one.astype(BF16)
        flux_one = ind_k == ((ind_l & 127) >> 5)
        flux_ind = jnp.concatenate(
            [(flux_one & (ind_l < 128)).astype(BF16), (flux_one & (ind_l >= 128)).astype(BF16)], axis=0
        )
        cf[...] = mdot(lhs[...], flux_ind).reshape(FIELDS, FIELDS, E_DEV, 256)

        low64 = iota((64, 128), 1) < 64
        blocks = []
        for d in range(3):
            padded = jnp.concatenate([stiff_ref[d], jnp.zeros((56, 72), F32)], axis=1)
            blocks.append(jnp.concatenate([twice(padded), jnp.zeros((8, 128), F32)], axis=0))
        for part, block in enumerate((jnp.where(low64, blocks[0], blocks[1]), blocks[2])):
            at = 128 * part
            hi, lo = hi_lo(block)
            vk[0:64, at : at + 128] = hi.astype(BF16)
            vk[64:128, at : at + 128] = hi.astype(BF16)
            vk[128:192, at : at + 128] = lo.astype(BF16)

        for i in range(4):
            sq[32 * i : 32 * i + 21, 0:56] = restrict_ref[i]
        traced = jnp.transpose(twice(sq[...]))
        store_rhs(rt, traced)
        for i in range(4):
            sq[32 * i : 32 * i + 21, 0:56] = lift_ref[i]
        hi, lo = hi_lo(twice(sq[...]))
        lf[0:128, :] = hi.astype(BF16)
        lf[128:256, :] = hi.astype(BF16)
        lf[256:384, :] = lo.astype(BF16)

        sq[...] = jnp.zeros_like(sq)
        for t in range(3):
            sq[21 * t : 21 * t + 21, 0:21] = orient_ref[t]
        turns = jnp.transpose(sq[...])[0:32, :]
        turns = (turns, pltpu.roll(turns, 64, 1))
        none = jnp.zeros((32, 128), F32)
        for nf in range(4):
            wide = [none, none]
            wide[nf // 2] = turns[nf % 2]
            hi, lo = hi_lo(jnp.concatenate(wide, axis=1))
            ob[32 * nf : 32 * nf + 32, :] = hi.astype(BF16)
            ob[128 + 32 * nf : 160 + 32 * nf, :] = hi.astype(BF16)
            ob[256 + 32 * nf : 288 + 32 * nf, :] = lo.astype(BF16)
        hi, lo = hi_lo(traced)
        hi, lo = hi.astype(BF16), lo.astype(BF16)
        store_rhs(qt, mdot(jnp.concatenate([hi, lo, hi], axis=1), ob[...]))

        perm16 = perm[:, 0:16]
        coded = []
        for i in range(4):
            coded.append(perm16 * slot_ref[i : i + 1, :].astype(F32))
        for i in range(4):
            coded.append(perm16 * face_ref[i : i + 1, :].astype(F32))
        for i in range(4):
            coded.append(perm16 * turn_ref[i : i + 1, :].astype(F32))
        coded.append(perm16 * rate_ref[...].astype(F32))
        codes_keep[...] = mdot(jnp.concatenate(coded, axis=0).astype(BF16), jnp.ones((16, 128), BF16))
        place_k = iota((256, 128), 0) & 63
        place_f = place_k - 21 * ((place_k >= 21).astype(jnp.int32) + (place_k >= 42).astype(jnp.int32))
        place_l = iota((256, 128), 1)
        for i in range(4):
            places[i] = ((place_l == place_f + 32 * i) & (place_k < 63)).astype(BF16)

    codes = codes_keep[...].astype(jnp.int32)
    slots, faces, turn_of = codes[0:64, 0:64], codes[64:128], codes[128:192]
    fast = codes[192:200, :] == 2
    ghost_slot = 16 + ((elem_lane & 3) ^ 1) * 4 + (elem_lane >> 2)
    target_row = jnp.where((lane16 & 16) > 0, ghost_slot, row)
    def tables(first, count):
        def part(values):
            return jnp.concatenate([values[16 * i + first : 16 * i + first + count] for i in range(4)], axis=0)

        slot_part, face_part, turn_part = part(slots), part(faces), part(turn_of)
        hot = (slot_part == jnp.broadcast_to(target_row[0:1, 0:64], (4 * count, 64))).astype(BF16)
        lane = iota((4 * count, 128), 1)
        inner = lane & 63
        turn_l = (inner >= 21).astype(jnp.int32) + (inner >= 42).astype(jnp.int32)
        mask = ((face_part & 1) == (lane >> 6)) & (turn_part == turn_l)
        return first, count, hot, face_part >= 2, mask.astype(F32)

    def own_terms(values):
        left = lhs_of(values)
        vol_keep[...] = couple_dirs(mdot(left, vk[...]).reshape(FIELDS, E_DEV, 256), ca, cb, E_DEV)
        own = mdot(left, rt[...]).reshape(FIELDS, E_DEV, 128)
        own_keep[...] = couple(own, lambda c: cf[c, :, :, 0:128])
        hi, lo = hi_lo(mdot(left, qt[...]).reshape(FIELDS, E_DEV, 256))
        zs[:, 0:16, :] = hi.astype(BF16)
        zs[:, 32:48, :] = lo.astype(BF16)

    def ghost_traces(ghosts, first):
        count = ghosts.shape[1]
        hi, lo = hi_lo(mdot(lhs_of(ghosts), qt[...]).reshape(FIELDS, count, 256))
        zs[:, 16 + first : 16 + first + count, :] = hi.astype(BF16)
        zs[:, 48 + first : 48 + first + count, :] = lo.astype(BF16)

    def advanced(table):
        first, count, hot, upper_face, mask = table
        cells = pl.ds(first, count)
        taken = []
        for c in range(FIELDS):
            one = mdot(hot, zs[c])
            taken.append(jnp.where(upper_face, one[:, 128:256], one[:, 0:128]) * mask)
        taken = jnp.stack(taken, axis=0)
        placed = None
        for i in range(4):
            hi, lo = hi_lo(taken[:, count * i : count * i + count, :].reshape(FIELDS * count, 128))
            one = mdot(jnp.concatenate([hi.astype(BF16), lo.astype(BF16)], axis=1), places[i])
            placed = one if placed is None else placed + one
        placed = placed.reshape(FIELDS, count, 128)
        flux = own_keep[:, cells, :] + couple(placed, lambda c: cf[c, :, cells, 128:256])
        hi, lo = hi_lo(flux.reshape(FIELDS * count, 128))
        hi, lo = hi.astype(BF16), lo.astype(BF16)
        lifted = mdot(jnp.concatenate([hi, lo, hi], axis=1), lf[...]).reshape(FIELDS, count, 128)
        return base_keep[:, cells, :] + vol_keep[:, cells, :] - lifted

    fast_rows, slow_rows, all_rows = tables(0, 8), tables(8, 8), tables(0, 16)
    own_terms(early)
    for copy in exchange_a:
        copy.wait()
    odd_row = (row8 & 1) == 1
    by_dom = jnp.where(odd_row, recv_a[0], recv_a[1])
    by_sub = jnp.where(odd_row, recv_a[2], recv_a[3])
    ghost8 = unpack(jnp.where(upper, by_dom, pltpu.roll(by_sub, 2, 1)))
    ghost16 = unpack(jnp.where(upper, pltpu.roll(by_dom, 6, 1), by_sub))
    ghost_traces(jnp.concatenate([ghost8, ghost16], axis=1), 0)
    current = advanced(fast_rows)
    base_keep[:, 0:8, :] = current
    restart = taylor_weight(0.0, 0.5, 0) * current
    for degree in range(1, DERIVS):
        current = derive(current)
        restart = restart + taylor_weight(0.0, 0.5, degree) * current
    late8 = jnp.where(fast[None], restart, late_keep[:, 0:8, :])

    fast_send(pack(late8), send_b)
    exchange_b = copies(lambda p: send_b.at[p // 2], recv_b, 2)
    for copy in exchange_b:
        copy.start()
    for copy in exchange_l:
        copy.wait()

    @pl.when(dom < n_dom)
    def _():
        base_keep[:, 8:16, :] = advanced(slow_rows)
        own_terms(jnp.concatenate([late8, late_keep[:, 8:16, :]], axis=1))
        ghost_traces(whole_ghosts(recv_l), 8)

    for copy in exchange_b:
        copy.wait()
    ghost_traces(fast_ghosts(recv_b), 0)
    final = advanced(all_rows)
    for c in range(FIELDS):
        out_ref[c] = permute(perm_back, final[c])[:, 0:56]


def solution(mesh):
    n_dom, n_sub = mesh.shape["dom"], mesh.shape["sub"]
    cells = (FIELDS, E_DEV, 128)

    def local(
        state,
        stiffness,
        star,
        face_restrict,
        face_lift,
        orient_maps,
        flux_local,
        flux_remote,
        cluster_rate,
        send_list,
        slot,
        face,
        turn,
    ):
        def entries(array):
            return jnp.transpose(array, (1, 2, 0, 3)).reshape(EVERY, array.shape[0], E_DEV)

        table = pltpu.VMEM((4, E_DEV), jnp.int32)
        out = pl.pallas_call(
            lambda *refs: kernel(n_dom, n_sub, *refs),
            out_shape=pltpu.VMEM((FIELDS, E_DEV, MODES), F32),
            in_specs=[pl.BlockSpec(memory_space=pltpu.HBM)] * 13,
            out_specs=pl.BlockSpec(memory_space=pltpu.VMEM),
            scratch_shapes=[
                pltpu.SMEM((1, 4, 4), jnp.int32),
                pltpu.VMEM((FIELDS, E_DEV, MODES), F32),
                pltpu.VMEM((3, MODES, MODES), F32),
                pltpu.VMEM((3, EVERY, E_DEV), F32),
                pltpu.VMEM((4, FACE_MODES, MODES), F32),
                pltpu.VMEM((4, FACE_MODES, MODES), F32),
                pltpu.VMEM((3, FACE_MODES, FACE_MODES), F32),
                pltpu.VMEM((4, EVERY, E_DEV), F32),
                pltpu.VMEM((4, EVERY, E_DEV), F32),
                pltpu.VMEM((1, E_DEV), jnp.int32),
                table,
                table,
                table,
                pltpu.SemaphoreType.DMA((27,)),
                pltpu.VMEM((192, 256), BF16),
                pltpu.VMEM((192, 256), BF16),
                pltpu.VMEM((192, 128), BF16),
                pltpu.VMEM((192, 256), BF16),
                pltpu.VMEM((384, 128), BF16),
                pltpu.VMEM((384, 256), BF16),
                pltpu.VMEM((128, 128), F32),
                pltpu.VMEM((256, 128), F32),
                pltpu.VMEM((88, 256), F32),
                pltpu.VMEM((EVERY * E_DEV, 256), BF16),
                pltpu.VMEM((FIELDS, FIELDS, E_DEV, 128), F32),
                pltpu.VMEM((FIELDS, 5, E_DEV, 128), F32),
                pltpu.VMEM((FIELDS, FIELDS, E_DEV, 256), F32),
                pltpu.VMEM((FIELDS, 64, 256), BF16),
                pltpu.VMEM((DERIVS - 1,) + cells, F32),
                pltpu.VMEM((208, 128), F32),
                pltpu.VMEM((4, 256, 128), BF16),
                pltpu.VMEM(cells, F32),
                pltpu.VMEM(cells, F32),
                pltpu.VMEM(cells, F32),
                pltpu.VMEM(cells, F32),
                pltpu.VMEM((2, 5, 8, 128), F32),
                pltpu.VMEM((5, 8, 128), F32),
                pltpu.VMEM((2, 3, 8, 128), F32),
                pltpu.VMEM((4, 5, 8, 128), F32),
                pltpu.VMEM((4, 5, 8, 128), F32),
                pltpu.VMEM((4, 3, 8, 128), F32),
                pltpu.SemaphoreType.DMA((3, 4)),
                pltpu.SemaphoreType.DMA((3, 4)),
            ],
            compiler_params=pltpu.CompilerParams(
                collective_id=0, has_side_effects=True
            ),
            name="ader_step",
        )(
            send_list,
            jnp.transpose(state, (1, 2, 0)),
            stiffness,
            entries(star),
            jnp.transpose(face_restrict, (1, 0, 2)),
            jnp.transpose(face_lift, (2, 0, 1)),
            orient_maps,
            entries(flux_local),
            entries(flux_remote),
            cluster_rate.reshape(1, E_DEV),
            slot,
            face,
            turn,
        )
        return jnp.transpose(out, (2, 0, 1))

    along = ("dom", "sub")
    placed = (
        P(None, None, along),
        P(),
        P(None, None, None, along),
        P(),
        P(),
        P(),
        P(None, None, None, along),
        P(None, None, None, along),
        P(along),
        P(along, None, None),
        P(None, along),
        P(None, along),
        P(None, along),
    )
    return jax.shard_map(
        local, mesh=mesh, in_specs=placed, out_specs=P(None, None, along), check_vma=False
    )
```
